32 devices in a mesh: param: 4 (over y, x), ex: 8 (over z, core).
Axes of the slice: x: 2, y: 2, z: 4, core: 2. Of those that a mesh axis runs over, the one named last changes fastest.
Arguments:
- activations: bfloat16 [64, 32, 4096], P('ex', None, 'param'), may hold values from -24 to 24
- output_gradients: bfloat16 [2, 64, 32, 4096], P(None, 'ex', None, 'param'), may hold values from -24 to 24
- down_projection_weight: bfloat16 [2, 16, 4096], P(None, None, 'param'), may hold values from -0.09375 to 0.09375
- adapter_up: bfloat16 [2, 4096, 16], P(None, 'param'), may hold values from -0.09375 to 0.09375
- projection: bfloat16 [262144, 4096], P(('param', 'ex')), may hold values from -0.111328125 to 0.111328125
- domains: int32 [64], P('ex'), may hold values from 0 to 3
- target_ids: int32 [256], P('param'), may hold values from 0 to 63
Outputs:
- scores: float32 [256, 64], P('param', 'ex')
- domain_scores: float32 [256, 4], P('param')
The draws below stay inside these ranges and needn't reach their ends.
All inputs are finite; a program needn't handle non-finite values.
Results may differ from the reference program's by a relative error of at most 0.0059.
Values may be sent and summed in bfloat16 or wider, within the bound.
No kernel may reach another device: no remote copies, remote signals or barrier semaphores. Data moves between devices by JAX's collectives and lax.ppermute only.
A program may use at most 192 MiB of HBM per device.

```python
import math
import jax
import jax.numpy as jnp
from jax import lax

D = 4096
R = 16
K = 4096
SEQ = 32
TGT = 256
DOMAINS = 4
N = 64
P_SIZE = 262144


def draw_activations(key, part):
    base = jax.random.truncated_normal(key, -4.0, 4.0, (N, SEQ, D), jnp.float32)
    level = jax.random.uniform(jax.random.fold_in(key, 7), (N, 1, 1), jnp.float32, 0.0, 0.5)
    return (base * 10.0 ** level).astype(jnp.bfloat16)


def draw_output_gradients(key, part):
    base = jax.random.truncated_normal(key, -4.0, 4.0, (2, N, SEQ, D), jnp.float32)
    level = jax.random.uniform(jax.random.fold_in(key, 11), (1, N, 1, 1), jnp.float32, 0.0, 0.5)
    return (base * 10.0 ** level).astype(jnp.bfloat16)


def draw_projection(key, part):
    column = jnp.arange(K, dtype=jnp.float32)[None, :] / K
    rough = jax.random.uniform(jax.random.fold_in(key, 5), (1, K), jnp.float32, -0.15, 0.15)
    spread = 10.0 ** (column + rough)
    base = jax.random.truncated_normal(key, -4.0, 4.0, (P_SIZE, K), jnp.float32)
    return (base * spread / jnp.sqrt(jnp.float32(P_SIZE))).astype(jnp.bfloat16)


def touch_ends(result, key, least, high):
    longest = result.shape.index(max(result.shape))
    spots = []
    for shift in (0, 1):
        where = [jax.random.randint(jax.random.fold_in(key, axis), (), 0, length) for axis, length in enumerate(result.shape)]
        where[longest] = (where[longest] + shift) % result.shape[longest]
        spots.append(tuple(where))
    return result.at[spots[0]].set(least).at[spots[1]].set(high)


def levels(stream_key, shape, shards, smallest, high):
    def one(dim, blocks):
        heights = jax.random.uniform(jax.random.fold_in(jax.random.fold_in(stream_key, 6), dim), (blocks,), jnp.float32, smallest / len(shards), high / len(shards))
        return jnp.repeat(jnp.exp(heights), shape[dim] // blocks).reshape((-1,) + (1,) * (len(shape) - dim - 1))

    loudness = one(*shards[0])
    for cut in shards[1:]:
        loudness = loudness * one(*cut)
    return loudness


def centred(stream_key, extent, deviation, reach, cuts=(), kind=jnp.bfloat16):
    array = jax.random.normal(stream_key, extent, jnp.float32) * deviation
    if len(cuts) > 0:
        array = levels(stream_key, extent, cuts, -0.22, 0.18) * array
    return jnp.clip(array, min=-reach, max=reach).astype(kind)


def setup_inputs(seed: int = 0) -> dict:
    key_of = jax.random.split(jax.random.key(seed), 8)
    activations = draw_activations(jax.random.fold_in(key_of[7], 71), 0)
    output_gradients = draw_output_gradients(jax.random.fold_in(key_of[7], 71), 0)
    down_projection_weight = centred(key_of[2], (2, R, D), D ** -0.5, 0.09375, ((2, 4),))
    adapter_up = centred(key_of[3], (2, D, R), D ** -0.5, 0.09375, ((1, 4),))
    projection = draw_projection(jax.random.fold_in(key_of[7], 71), 0)
    domains = touch_ends(jax.random.randint(key_of[5], (N,), 0, DOMAINS), jax.random.fold_in(key_of[5], 1), 0, DOMAINS - 1).astype(jnp.int32)
    target_ids = touch_ends(jax.random.randint(key_of[6], (TGT,), 0, N), jax.random.fold_in(key_of[6], 1), 0, N - 1).astype(jnp.int32)
    return dict(activations=activations, output_gradients=output_gradients, down_projection_weight=down_projection_weight, adapter_up=adapter_up, projection=projection, domains=domains, target_ids=target_ids)


def reference(activations, output_gradients, down_projection_weight, adapter_up, projection, domains, target_ids):
    single_float = jnp.float32
    up_terms = jnp.einsum('ansd,adr->ansr', output_gradients.astype(single_float), adapter_up.astype(single_float))
    down_terms = jnp.einsum('nsd,ard->ansr', activations.astype(single_float), down_projection_weight.astype(single_float))
    rank_factor = jnp.concatenate([up_terms[0], up_terms[1], down_terms[0], down_terms[1]], axis=-1).astype(jnp.bfloat16)
    low_float = rank_factor.astype(single_float)
    block_width = math.gcd(D, 256)
    block_count = D // block_width
    channels = 4 * R

    def accumulate(total, index):
        start = (index * block_width).astype(jnp.int32)
        inputs = lax.dynamic_slice_in_dim(activations, start, block_width, 2).astype(single_float)
        grad_block = lax.dynamic_slice_in_dim(output_gradients, start, block_width, 3).astype(single_float)
        first = jnp.einsum('erb,ery->eby', inputs, low_float[..., :2 * R])
        second = jnp.einsum('fai,fav->fiv', grad_block[0], low_float[..., 2 * R:3 * R])
        third = jnp.einsum('fai,fav->fiv', grad_block[1], low_float[..., 3 * R:])
        grads = jnp.concatenate([first, second, third], axis=-1).astype(jnp.bfloat16)
        grads = grads.reshape(N, block_width * channels).astype(single_float)
        rows = lax.dynamic_slice_in_dim(projection, (start * channels).astype(jnp.int32), block_width * channels, 0).astype(single_float)
        return (total + jnp.dot(grads, rows, preferred_element_type=single_float), None)
    features, _ = lax.scan(accumulate, jnp.zeros((N, K), single_float), jnp.arange(block_count, dtype=jnp.int32))
    unit_rows = features * lax.rsqrt(lax.optimization_barrier(jnp.sum(features * features, axis=1)) + 1e-06)[:, None]
    gram = jnp.dot(unit_rows, unit_rows.T, precision=lax.Precision.HIGHEST, preferred_element_type=single_float)
    kernel = gram + 0.25 * jnp.eye(N, dtype=single_float)
    lower = jnp.linalg.cholesky(kernel)
    cross = jnp.take(gram, target_ids, axis=0)
    selfmask = target_ids[:, None] == jnp.arange(N, dtype=jnp.int32)[None, :]
    cross = jnp.where(selfmask, jnp.zeros_like(cross), cross)
    solved = jax.scipy.linalg.cho_solve((lower, True), cross.T)
    scores = math.sqrt(K) * solved.T
    indicator_matrix = (domains[:, None] == jnp.arange(DOMAINS, dtype=jnp.int32)[None, :]).astype(single_float)
    domain_scores = jnp.dot(scores, indicator_matrix, precision=lax.Precision.HIGHEST, preferred_element_type=single_float) / math.sqrt(N / DOMAINS)
    return (scores, domain_scores)
```

```python
import math

import jax
import jax.numpy as jnp
from jax import lax
from jax.sharding import PartitionSpec as P

K = 4096
DOMAINS = 4
EVERY = ("param", "ex")


def exact_dot(left, right, dims):
    return lax.dot_general(
        left, right, (dims, ((), ())), precision=lax.Precision.HIGHEST, preferred_element_type=jnp.float32
    )


def swap(blocks, axes):
    return lax.all_to_all(blocks, axes, split_axis=0, concat_axis=0, tiled=True)


def local(
    activations,
    output_gradients,
    down_projection_weight,
    adapter_up,
    projection,
    domains,
    target_ids,
):
    single_float = jnp.float32
    ex_rows = activations.shape[0]
    rank = down_projection_weight.shape[1]
    ex_size = lax.axis_size("ex")
    devices = lax.axis_size("param") * ex_size
    example_count = ex_rows * ex_size

    up_terms = jnp.einsum(
        "ansd,adr->ansr", output_gradients, adapter_up, preferred_element_type=single_float
    )
    down_terms = jnp.einsum(
        "nsd,ard->ansr", activations, down_projection_weight, preferred_element_type=single_float
    )
    partial_low = jnp.concatenate([up_terms[0], up_terms[1], down_terms[0], down_terms[1]], axis=-1)
    low = jnp.sum(lax.all_gather(partial_low, "param"), axis=0).astype(jnp.bfloat16)

    first = jnp.einsum(
        "erb,ery->eby", activations, low[..., : 2 * rank], preferred_element_type=single_float
    )
    second = jnp.einsum(
        "fai,fav->fiv",
        output_gradients[0],
        low[..., 2 * rank : 3 * rank],
        preferred_element_type=single_float,
    )
    third = jnp.einsum(
        "fai,fav->fiv", output_gradients[1], low[..., 3 * rank :], preferred_element_type=single_float
    )
    grads = jnp.concatenate([first, second, third], axis=-1).astype(jnp.bfloat16)
    grads = grads.reshape(ex_rows, grads.shape[1] * grads.shape[2])
    grads = lax.all_to_all(grads, "ex", split_axis=1, concat_axis=0, tiled=True)

    partial_features = jnp.dot(grads, projection, preferred_element_type=single_float)
    blocks = partial_features.astype(jnp.bfloat16).reshape(example_count, devices, K // devices)
    features = jnp.sum(swap(blocks.transpose(1, 0, 2), EVERY).astype(single_float).reshape(
        devices, example_count, K // devices), axis=0)

    raw_gram = exact_dot(features, features, ((1,), (1,)))
    rows = example_count // devices
    raw_rows = jnp.sum(swap(raw_gram, EVERY).reshape(devices, rows, example_count), axis=0)
    domain_row = jnp.pad(domains.astype(single_float), (0, example_count - ex_rows))
    piece = jnp.concatenate([raw_rows, domain_row[None]], axis=0)
    pieces = swap(jnp.broadcast_to(piece[None], (devices, rows + 1, example_count)), EVERY)
    raw_gram = pieces[:, :rows].reshape(example_count, example_count)
    all_domains = pieces[:ex_size, rows, :ex_rows].reshape(example_count).astype(jnp.int32)

    eye = jnp.eye(example_count, dtype=single_float)
    inverse_norm = lax.rsqrt(jnp.sum(raw_gram * eye, axis=0) + 1e-06)
    gram = raw_gram * inverse_norm[:, None] * inverse_norm[None, :]
    lower = jnp.linalg.cholesky(gram + 0.25 * eye)
    inverse = jax.scipy.linalg.cho_solve((lower, True), eye)
    cross = jnp.take(gram, target_ids, axis=0)
    selfmask = target_ids[:, None] == jnp.arange(example_count, dtype=jnp.int32)[None, :]
    cross = jnp.where(selfmask, jnp.zeros_like(cross), cross)
    scores = math.sqrt(K) * exact_dot(cross, inverse, ((1,), (0,)))
    indicator = (all_domains[:, None] == jnp.arange(DOMAINS, dtype=jnp.int32)[None, :]).astype(single_float)
    domain_scores = exact_dot(scores, indicator, ((1,), (0,))) / math.sqrt(example_count / DOMAINS)
    first_row = lax.axis_index("ex") * ex_rows
    return (lax.dynamic_slice_in_dim(scores, first_row, ex_rows, axis=1), domain_scores)


def solution(mesh):
    in_specs = (
        P("ex", None, "param"),
        P(None, "ex", None, "param"),
        P(None, None, "param"),
        P(None, "param", None),
        P(("param", "ex"), None),
        P("ex"),
        P("param"),
    )
    out_specs = (P("param", "ex"), P("param", None))
    return jax.shard_map(local, mesh=mesh, in_specs=in_specs, out_specs=out_specs, check_vma=False)
```

```python
import functools
import math

import jax
import jax.numpy as jnp
from jax import lax
from jax.experimental import pallas as pl
from jax.experimental.pallas import tpu as pltpu
from jax.sharding import PartitionSpec as P

K = 4096
DOMAINS = 4
HALF = 32
EVERY = ("param", "ex")


def exact_dot(left, right, dims):
    return lax.dot_general(
        left, right, (dims, ((), ())), precision=lax.Precision.HIGHEST, preferred_element_type=jnp.float32
    )


def swap(blocks, axes):
    return lax.all_to_all(blocks, axes, split_axis=0, concat_axis=0, tiled=True)


def packs(example_count):
    return example_count == 2 * HALF


def packed_gram_kernel(blocks_ref, row_ref, out_ref):
    features = jnp.sum(blocks_ref[...].astype(jnp.float32), axis=0)
    gram = exact_dot(features, features, ((1,), (1,)))
    upper, across, under = gram[:HALF, :HALF], gram[:HALF, HALF:], gram[HALF:, HALF:]
    rows = lax.broadcasted_iota(jnp.int32, (HALF, HALF), 0)
    cols = lax.broadcasted_iota(jnp.int32, (HALF, HALF), 1)
    mixed = jnp.where(rows <= cols, upper, under)
    quarter = HALF // 2
    body = jnp.concatenate([across[:quarter], across[quarter:], mixed[:quarter], mixed[quarter:]], axis=1)
    diagonal = jnp.sum(jnp.where(rows == cols, under, 0.0), axis=0, keepdims=True)
    last = row_ref[...] + jnp.concatenate([diagonal, jnp.zeros((1, 128 - HALF), jnp.float32)], axis=1)
    piece = jnp.concatenate([body, jnp.broadcast_to(last, (8, 128))], axis=0)
    out_ref[...] = jnp.broadcast_to(piece[None], out_ref.shape)


def packed_gram(blocks, row):
    return pl.pallas_call(
        packed_gram_kernel,
        out_shape=jax.ShapeDtypeStruct((blocks.shape[0], HALF // 2 + 8, 128), jnp.float32),
        name="packed_gram",
    )(blocks, row)


def unpack(total):
    quarter = HALF // 2
    rows = lax.broadcasted_iota(jnp.int32, (HALF, HALF), 0)
    cols = lax.broadcasted_iota(jnp.int32, (HALF, HALF), 1)
    body = total[:quarter]
    across = jnp.concatenate([body[:, :HALF], body[:, HALF : 2 * HALF]], axis=0)
    mixed = jnp.concatenate([body[:, 2 * HALF : 3 * HALF], body[:, 3 * HALF :]], axis=0)
    turned = mixed.T
    upper = jnp.where(rows <= cols, mixed, turned)
    diagonal = jnp.broadcast_to(total[quarter : quarter + 1, :HALF], (HALF, HALF))
    under = jnp.where(rows == cols, diagonal, jnp.where(rows > cols, mixed, turned))
    gram = jnp.concatenate(
        [jnp.concatenate([upper, across], axis=1), jnp.concatenate([across.T, under], axis=1)], axis=0
    )
    return gram, total[quarter : quarter + 1, HALF : 3 * HALF]


def solve_kernel(count, slot_ref, pieces_ref, ids_ref, scores_ref, domain_ref, work_ref):
    total = jnp.sum(pieces_ref[...], axis=0)
    if packs(count):
        raw_gram, all_domains = unpack(total)
    else:
        raw_gram, all_domains = total[:count], total[count : count + 1]
    rows = lax.broadcasted_iota(jnp.int32, (count, count), 0)
    cols = lax.broadcasted_iota(jnp.int32, (count, count), 1)
    on_diagonal = jnp.where(rows == cols, raw_gram, 0.0)
    gram = raw_gram * lax.rsqrt(jnp.sum(on_diagonal, axis=1, keepdims=True) + 1e-06)
    gram = gram * lax.rsqrt(jnp.sum(on_diagonal, axis=0, keepdims=True) + 1e-06)

    work_ref[...] = gram + jnp.where(rows == cols, 0.25, 0.0)

    def sweep(k, carry):
        held = work_ref[...]
        row = work_ref[pl.ds(k, 1), :]
        pivot = 1.0 / jnp.sum(jnp.where(cols[:1] == k, row, 0.0), axis=1, keepdims=True)
        column = jnp.sum(jnp.where(cols == k, held, 0.0), axis=1, keepdims=True)
        row = jnp.where(cols[:1] == k, -pivot, row * pivot)
        column = jnp.where(rows[:, :1] == k, -1.0, column)
        work_ref[...] = jnp.where((cols == k) | (rows == k), 0.0, held) - column * row
        return carry

    lax.fori_loop(0, count, sweep, 0)

    targets = ids_ref.shape[1]
    places = lax.broadcasted_iota(jnp.int32, (count, targets), 0)
    chosen = places == ids_ref[...]
    cross = exact_dot(gram, jnp.where(chosen, 1.0, 0.0), ((1,), (0,)))
    cross = jnp.where(chosen, 0.0, cross)
    scores = exact_dot(work_ref[...], cross, ((1,), (0,))) * -math.sqrt(K)
    kinds = lax.broadcasted_iota(jnp.int32, (DOMAINS, count), 0).astype(jnp.float32)
    indicator = jnp.where(kinds == all_domains, 1.0, 0.0)
    domain_ref[...] = exact_dot(indicator, scores, ((1,), (0,))) / math.sqrt(count / DOMAINS)
    work_ref[:, :targets] = scores
    scores_ref[...] = work_ref[pl.ds(pl.multiple_of(slot_ref[0], 8), scores_ref.shape[0]), :targets]


def solve(pieces, target_ids, slot, ex_rows, count):
    targets = target_ids.shape[0]
    return pl.pallas_call(
        functools.partial(solve_kernel, count),
        out_shape=(
            jax.ShapeDtypeStruct((ex_rows, targets), jnp.float32),
            jax.ShapeDtypeStruct((DOMAINS, targets), jnp.float32),
        ),
        in_specs=[
            pl.BlockSpec(memory_space=pltpu.SMEM),
            pl.BlockSpec(memory_space=pltpu.VMEM),
            pl.BlockSpec(memory_space=pltpu.VMEM),
        ],
        out_specs=(pl.BlockSpec(memory_space=pltpu.VMEM), pl.BlockSpec(memory_space=pltpu.VMEM)),
        scratch_shapes=[pltpu.VMEM((count, count), jnp.float32)],
        name="solve",
    )(jnp.reshape(slot, (1,)), pieces, target_ids[None])


def local(
    activations,
    output_gradients,
    down_projection_weight,
    adapter_up,
    projection,
    domains,
    target_ids,
):
    single_float = jnp.float32
    ex_rows = activations.shape[0]
    rank = down_projection_weight.shape[1]
    ex_size = lax.axis_size("ex")
    devices = lax.axis_size("param") * ex_size
    example_count = ex_rows * ex_size

    up_terms = jnp.einsum(
        "ansd,adr->ansr", output_gradients, adapter_up, preferred_element_type=single_float
    )
    down_terms = jnp.einsum(
        "nsd,ard->ansr", activations, down_projection_weight, preferred_element_type=single_float
    )
    partial_low = jnp.concatenate([up_terms[0], up_terms[1], down_terms[0], down_terms[1]], axis=-1)
    low = jnp.sum(lax.all_gather(partial_low, "param"), axis=0).astype(jnp.bfloat16)

    first = jnp.einsum(
        "erb,ery->eby", activations, low[..., : 2 * rank], preferred_element_type=single_float
    )
    second = jnp.einsum(
        "fai,fav->fiv",
        output_gradients[0],
        low[..., 2 * rank : 3 * rank],
        preferred_element_type=single_float,
    )
    third = jnp.einsum(
        "fai,fav->fiv", output_gradients[1], low[..., 3 * rank :], preferred_element_type=single_float
    )
    grads = jnp.concatenate([first, second, third], axis=-1).astype(jnp.bfloat16)
    grads = grads.reshape(ex_rows, grads.shape[1] * grads.shape[2])
    grads = lax.all_to_all(grads, "ex", split_axis=1, concat_axis=0, tiled=True)

    partial_features = jnp.dot(grads, projection, preferred_element_type=single_float)
    blocks = partial_features.astype(jnp.bfloat16).reshape(example_count, devices, K // devices)
    arrived = swap(blocks.transpose(1, 0, 2), EVERY)

    slot = lax.axis_index("ex") * ex_rows
    mine = jnp.where(lax.axis_index("param") == 0, domains, 0).astype(single_float)
    domain_row = lax.dynamic_update_slice(jnp.zeros((example_count,), single_float), mine, (slot,))
    if packs(example_count):
        row = jnp.pad(domain_row, (HALF, 128 - HALF - example_count))[None]
        pieces = swap(packed_gram(arrived, row), EVERY)
    else:
        features = jnp.sum(arrived.astype(single_float), axis=0)
        gram = exact_dot(features, features, ((1,), (1,)))
        gram = jnp.concatenate([gram, jnp.broadcast_to(domain_row, (devices, example_count))], axis=0)
        share = gram.shape[0] // devices
        summed = jnp.sum(swap(gram, EVERY).reshape(devices, share, example_count), axis=0)
        pieces = swap(jnp.broadcast_to(summed[None], (devices, share, example_count)), EVERY)
        pieces = pieces.reshape(1, devices * share, example_count)
    scores, domain_scores = solve(pieces, target_ids, slot, ex_rows, example_count)
    return (scores.T, domain_scores.T)


def solution(mesh):
    in_specs = (
        P("ex", None, "param"),
        P(None, "ex", None, "param"),
        P(None, None, "param"),
        P(None, "param", None),
        P(("param", "ex"), None),
        P("ex"),
        P("param"),
    )
    out_specs = (P("param", "ex"), P("param", None))
    return jax.shard_map(local, mesh=mesh, in_specs=in_specs, out_specs=out_specs, check_vma=False)
```

```python
import functools
import math

import jax
import jax.numpy as jnp
from jax import lax
from jax.experimental import pallas as pl
from jax.experimental.pallas import tpu as pltpu
from jax.sharding import PartitionSpec as P

K = 4096
DOMAINS = 4
HALF = 32
EARLY = 9
BLOCK = 256
SLOTS = 12
EVERY = ("param", "ex")


def exact_dot(left, right, dims):
    return lax.dot_general(
        left, right, (dims, ((), ())), precision=lax.Precision.HIGHEST, preferred_element_type=jnp.float32
    )


def swap(blocks, axes):
    return lax.all_to_all(blocks, axes, split_axis=0, concat_axis=0, tiled=True)


def gradient_rows_kernel(early, act_in, out_in, low_ref, first_ref, second_ref, act_ref, out_ref, tall_ref, wide_ref, sems):
    copies = [pltpu.make_async_copy(act_in, act_ref, sems.at[0]), pltpu.make_async_copy(out_in, out_ref, sems.at[1])]
    for copy in copies:
        copy.start()
    examples, _, channels = act_ref.shape
    rank = low_ref.shape[3] // 4
    blocks = first_ref.shape[0]
    low = low_ref[0]
    for part in range(1, low_ref.shape[0]):
        low = low + low_ref[part]
    low = low.astype(jnp.bfloat16).astype(jnp.float32)
    for copy in copies:
        copy.wait()
    for n in range(examples):
        twice = jnp.concatenate([low[n], low[n]], axis=1)
        lane = lax.broadcasted_iota(jnp.int32, twice.shape, 1)
        column = lax.rem(lane, 4 * rank)
        factors = jnp.concatenate(
            [
                jnp.where(column < 2 * rank, twice, 0.0),
                jnp.where((column >= 2 * rank) & (column < 3 * rank), twice, 0.0),
                jnp.where(column >= 3 * rank, twice, 0.0),
            ],
            axis=0,
        ).astype(jnp.bfloat16)
        tokens = jnp.concatenate([act_ref[n], out_ref[0, n], out_ref[1, n]], axis=0)
        tall_ref[...] = lax.dot_general(
            tokens, factors, (((0,), (0,)), ((), ())), preferred_element_type=jnp.float32
        )
        even = tall_ref[pl.ds(0, channels // 2, stride=2), :]
        odd = tall_ref[pl.ds(1, channels // 2, stride=2), :]
        lane = lax.broadcasted_iota(jnp.int32, even.shape, 1)
        wide_ref[pl.ds(n, channels // 2, stride=examples), :] = jnp.where(lane < 4 * rank, even, odd)
    tiles = channels // 2 // blocks
    for block in range(blocks):
        for tile in range(tiles):
            start = (block * tiles + tile) * examples
            piece = wide_ref[start : start + examples, :].astype(jnp.bfloat16)
            at = tile * 128
            if at < early:
                first_ref[block, :, at : at + 128] = piece
            else:
                second_ref[block, :, at - early : at - early + 128] = piece


def gradient_rows(activations, output_gradients, low_parts, blocks, early):
    examples, _, channels = activations.shape
    columns = low_parts.shape[3]
    lanes = channels * columns // blocks
    return pl.pallas_call(
        functools.partial(gradient_rows_kernel, early),
        out_shape=(
            jax.ShapeDtypeStruct((blocks, examples, early), jnp.bfloat16),
            jax.ShapeDtypeStruct((blocks, examples, lanes - early), jnp.bfloat16),
        ),
        in_specs=[
            pl.BlockSpec(memory_space=pl.ANY),
            pl.BlockSpec(memory_space=pl.ANY),
            pl.BlockSpec(memory_space=pltpu.VMEM),
        ],
        scratch_shapes=[
            pltpu.VMEM(activations.shape, activations.dtype),
            pltpu.VMEM(output_gradients.shape, output_gradients.dtype),
            pltpu.VMEM((channels, 2 * columns), jnp.float32),
            pltpu.VMEM((channels // 2 * examples, 2 * columns), jnp.float32),
            pltpu.SemaphoreType.DMA((2,)),
        ],
        compiler_params=pltpu.CompilerParams(vmem_limit_bytes=24 << 20),
        name="gradient_rows",
    )(activations, output_gradients, low_parts)


def partial_features_kernel(first_row, has_total, *refs):
    if has_total:
        grads_ref, rows_ref, total_ref, out_ref, acc_ref, held_ref, sems = refs
    else:
        grads_ref, rows_ref, out_ref, held_ref, sems = refs
        acc_ref = out_ref
    slots, block, _ = held_ref.shape
    count = grads_ref.shape[1]
    starts = list(range(0, count, block))

    def copy(i):
        size = min(block, count - starts[i])
        return pltpu.make_async_copy(
            rows_ref.at[pl.ds(first_row + starts[i], size)],
            held_ref.at[i % slots, pl.ds(0, size)],
            sems.at[i % slots],
        )

    for i in range(min(slots, len(starts))):
        copy(i).start()
    for i, start in enumerate(starts):
        size = min(block, count - start)
        copy(i).wait()
        product = jnp.dot(
            grads_ref[:, start : start + size], held_ref[i % slots, :size], preferred_element_type=jnp.float32
        )
        if i:
            acc_ref[...] += product
        elif has_total:
            acc_ref[...] = total_ref[...] + product
        else:
            acc_ref[...] = product
        if i + slots < len(starts):
            copy(i + slots).start()
    if has_total:
        if len(out_ref.shape) == 3:
            lanes = out_ref.shape[2]
            for block in range(out_ref.shape[0]):
                out_ref[block] = acc_ref[:, block * lanes : (block + 1) * lanes].astype(out_ref.dtype)
        else:
            out_ref[...] = acc_ref[...].astype(out_ref.dtype)


def partial_features(grads, projection, first_row, total, blocks):
    examples, count = grads.shape
    columns = projection.shape[1]
    in_vmem = pl.BlockSpec(memory_space=pltpu.VMEM)
    in_specs = [in_vmem, pl.BlockSpec(memory_space=pl.ANY)]
    scratch = [pltpu.VMEM((SLOTS, BLOCK, columns), projection.dtype), pltpu.SemaphoreType.DMA((SLOTS,))]
    operands = (grads, projection)
    out_shape = jax.ShapeDtypeStruct((examples, columns), jnp.float32)
    if total is not None:
        operands += (total,)
        in_specs.append(in_vmem)
        scratch.insert(0, pltpu.VMEM((examples, columns), jnp.float32))
        shape = (examples, columns) if columns // blocks % 128 else (blocks, examples, columns // blocks)
        out_shape = jax.ShapeDtypeStruct(shape, jnp.bfloat16)
    return pl.pallas_call(
        functools.partial(partial_features_kernel, first_row, total is not None),
        out_shape=out_shape,
        in_specs=in_specs,
        out_specs=in_vmem,
        scratch_shapes=scratch,
        compiler_params=pltpu.CompilerParams(vmem_limit_bytes=40 << 20),
        name="partial_features",
    )(*operands)


def packs(example_count):
    return example_count == 2 * HALF


def packed_gram_kernel(blocks_ref, row_ref, out_ref):
    features = jnp.sum(blocks_ref[...].astype(jnp.float32), axis=0)
    gram = exact_dot(features, features, ((1,), (1,)))
    upper, across, under = gram[:HALF, :HALF], gram[:HALF, HALF:], gram[HALF:, HALF:]
    rows = lax.broadcasted_iota(jnp.int32, (HALF, HALF), 0)
    cols = lax.broadcasted_iota(jnp.int32, (HALF, HALF), 1)
    mixed = jnp.where(rows <= cols, upper, under)
    quarter = HALF // 2
    body = jnp.concatenate([across[:quarter], across[quarter:], mixed[:quarter], mixed[quarter:]], axis=1)
    diagonal = jnp.sum(jnp.where(rows == cols, under, 0.0), axis=0, keepdims=True)
    last = row_ref[...] + jnp.concatenate([diagonal, jnp.zeros((1, 128 - HALF), jnp.float32)], axis=1)
    piece = jnp.concatenate([body, jnp.broadcast_to(last, (8, 128))], axis=0)
    out_ref[...] = jnp.broadcast_to(piece[None], out_ref.shape)


def packed_gram(blocks, row):
    return pl.pallas_call(
        packed_gram_kernel,
        out_shape=jax.ShapeDtypeStruct((blocks.shape[0], HALF // 2 + 8, 128), jnp.float32),
        compiler_params=pltpu.CompilerParams(vmem_limit_bytes=16 << 20),
        name="packed_gram",
    )(blocks, row)


def unpack(total):
    quarter = HALF // 2
    rows = lax.broadcasted_iota(jnp.int32, (HALF, HALF), 0)
    cols = lax.broadcasted_iota(jnp.int32, (HALF, HALF), 1)
    body = total[:quarter]
    across = jnp.concatenate([body[:, :HALF], body[:, HALF : 2 * HALF]], axis=0)
    mixed = jnp.concatenate([body[:, 2 * HALF : 3 * HALF], body[:, 3 * HALF :]], axis=0)
    turned = mixed.T
    upper = jnp.where(rows <= cols, mixed, turned)
    diagonal = jnp.broadcast_to(total[quarter : quarter + 1, :HALF], (HALF, HALF))
    under = jnp.where(rows == cols, diagonal, jnp.where(rows > cols, mixed, turned))
    gram = jnp.concatenate(
        [jnp.concatenate([upper, across], axis=1), jnp.concatenate([across.T, under], axis=1)], axis=0
    )
    return gram, total[quarter : quarter + 1, HALF : 3 * HALF]


def solve_kernel(count, slot_ref, pieces_ref, ids_ref, scores_ref, domain_ref, work_ref):
    total = jnp.sum(pieces_ref[...], axis=0)
    if packs(count):
        raw_gram, all_domains = unpack(total)
    else:
        raw_gram, all_domains = total[:count], total[count : count + 1]
    rows = lax.broadcasted_iota(jnp.int32, (count, count), 0)
    cols = lax.broadcasted_iota(jnp.int32, (count, count), 1)
    on_diagonal = jnp.where(rows == cols, raw_gram, 0.0)
    gram = raw_gram * lax.rsqrt(jnp.sum(on_diagonal, axis=1, keepdims=True) + 1e-06)
    gram = gram * lax.rsqrt(jnp.sum(on_diagonal, axis=0, keepdims=True) + 1e-06)

    work_ref[...] = gram + jnp.where(rows == cols, 0.25, 0.0)

    def sweep(k, carry):
        held = work_ref[...]
        row = work_ref[pl.ds(k, 1), :]
        pivot = 1.0 / jnp.sum(jnp.where(cols[:1] == k, row, 0.0), axis=1, keepdims=True)
        column = jnp.sum(jnp.where(cols == k, held, 0.0), axis=1, keepdims=True)
        row = jnp.where(cols[:1] == k, -pivot, row * pivot)
        column = jnp.where(rows[:, :1] == k, -1.0, column)
        work_ref[...] = jnp.where((cols == k) | (rows == k), 0.0, held) - column * row
        return carry

    lax.fori_loop(0, count, sweep, 0)

    targets = ids_ref.shape[1]
    places = lax.broadcasted_iota(jnp.int32, (count, targets), 0)
    chosen = places == ids_ref[...]
    cross = exact_dot(gram, jnp.where(chosen, 1.0, 0.0), ((1,), (0,)))
    cross = jnp.where(chosen, 0.0, cross)
    scores = exact_dot(work_ref[...], cross, ((1,), (0,))) * -math.sqrt(K)
    kinds = lax.broadcasted_iota(jnp.int32, (DOMAINS, count), 0).astype(jnp.float32)
    indicator = jnp.where(kinds == all_domains, 1.0, 0.0)
    domain_ref[...] = exact_dot(indicator, scores, ((1,), (0,))) / math.sqrt(count / DOMAINS)
    work_ref[:, :targets] = scores
    scores_ref[...] = work_ref[pl.ds(pl.multiple_of(slot_ref[0], 8), scores_ref.shape[0]), :targets]


def solve(pieces, target_ids, slot, ex_rows, count):
    targets = target_ids.shape[0]
    return pl.pallas_call(
        functools.partial(solve_kernel, count),
        out_shape=(
            jax.ShapeDtypeStruct((ex_rows, targets), jnp.float32),
            jax.ShapeDtypeStruct((DOMAINS, targets), jnp.float32),
        ),
        in_specs=[
            pl.BlockSpec(memory_space=pltpu.SMEM),
            pl.BlockSpec(memory_space=pltpu.VMEM),
            pl.BlockSpec(memory_space=pltpu.VMEM),
        ],
        out_specs=(pl.BlockSpec(memory_space=pltpu.VMEM), pl.BlockSpec(memory_space=pltpu.VMEM)),
        scratch_shapes=[pltpu.VMEM((count, count), jnp.float32)],
        compiler_params=pltpu.CompilerParams(vmem_limit_bytes=16 << 20),
        name="solve",
    )(jnp.reshape(slot, (1,)), pieces, target_ids[None])


def local(
    activations,
    output_gradients,
    down_projection_weight,
    adapter_up,
    projection,
    domains,
    target_ids,
):
    single_float = jnp.float32
    ex_rows = activations.shape[0]
    rank = down_projection_weight.shape[1]
    ex_size = lax.axis_size("ex")
    devices = lax.axis_size("param") * ex_size
    example_count = ex_rows * ex_size

    up_terms = jnp.einsum(
        "ansd,adr->ansr", output_gradients, adapter_up, preferred_element_type=single_float
    )
    down_terms = jnp.einsum(
        "nsd,ard->ansr", activations, down_projection_weight, preferred_element_type=single_float
    )
    partial_low = jnp.concatenate([up_terms[0], up_terms[1], down_terms[0], down_terms[1]], axis=-1)
    low_parts = lax.all_gather(partial_low, "param")

    row_count = projection.shape[0]
    early = row_count * EARLY // (16 * 128) * 128
    wires = gradient_rows(activations, output_gradients, low_parts, ex_size, early)
    arrived = [swap(wire, "ex").reshape(example_count, wire.shape[2]) for wire in wires]
    total = partial_features(arrived[0], projection, 0, None, 1)
    partial_sums = partial_features(arrived[1], projection, early, total, devices)
    if partial_sums.ndim == 2:
        partial_sums = partial_sums.reshape(example_count, devices, K // devices).transpose(1, 0, 2)
    arrived = swap(partial_sums, EVERY)

    slot = lax.axis_index("ex") * ex_rows
    mine = jnp.where(lax.axis_index("param") == 0, domains, 0).astype(single_float)
    domain_row = lax.dynamic_update_slice(jnp.zeros((example_count,), single_float), mine, (slot,))
    if packs(example_count):
        row = jnp.pad(domain_row, (HALF, 128 - HALF - example_count))[None]
        pieces = swap(packed_gram(arrived, row), EVERY)
    else:
        features = jnp.sum(arrived.astype(single_float), axis=0)
        gram = exact_dot(features, features, ((1,), (1,)))
        gram = jnp.concatenate([gram, jnp.broadcast_to(domain_row, (devices, example_count))], axis=0)
        share = gram.shape[0] // devices
        summed = jnp.sum(swap(gram, EVERY).reshape(devices, share, example_count), axis=0)
        pieces = swap(jnp.broadcast_to(summed[None], (devices, share, example_count)), EVERY)
        pieces = pieces.reshape(1, devices * share, example_count)
    scores, domain_scores = solve(pieces, target_ids, slot, ex_rows, example_count)
    return (scores.T, domain_scores.T)


def solution(mesh):
    in_specs = (
        P("ex", None, "param"),
        P(None, "ex", None, "param"),
        P(None, None, "param"),
        P(None, "param", None),
        P(("param", "ex"), None),
        P("ex"),
        P("param"),
    )
    out_specs = (P("param", "ex"), P("param", None))
    return jax.shard_map(local, mesh=mesh, in_specs=in_specs, out_specs=out_specs, check_vma=False)
```

```python
import functools
import math

import jax
import jax.numpy as jnp
from jax import lax
from jax.experimental import pallas as pl
from jax.experimental.pallas import tpu as pltpu
from jax.sharding import PartitionSpec as P

K = 4096
DOMAINS = 4
HALF = 32
FOLD = 4
GROUP = 8
SLOTS = 12
EVERY = ("param", "ex")


def exact_dot(left, right, dims):
    return lax.dot_general(
        left, right, (dims, ((), ())), precision=lax.Precision.HIGHEST, preferred_element_type=jnp.float32
    )


def swap(blocks, axes):
    return lax.all_to_all(blocks, axes, split_axis=0, concat_axis=0, tiled=True)


def spread(columns):
    return jnp.concatenate([columns] * FOLD, axis=0).T


def low_columns_kernel(parts_ref, queries_ref, rest_ref):
    low = parts_ref[0]
    for part in range(1, parts_ref.shape[0]):
        low = low + parts_ref[part]
    low = low.astype(jnp.bfloat16)
    half = low.shape[0] // 2
    for block in range(queries_ref.shape[0]):
        queries_ref[block] = low[:half]
    rest_ref[...] = spread(low[half:].astype(jnp.float32)).astype(jnp.bfloat16)


def low_columns(parts, blocks):
    _, columns, tokens = parts.shape
    return pl.pallas_call(
        low_columns_kernel,
        out_shape=(
            jax.ShapeDtypeStruct((blocks, columns // 2, tokens), jnp.bfloat16),
            jax.ShapeDtypeStruct((tokens, FOLD * columns // 2), jnp.bfloat16),
        ),
        compiler_params=pltpu.CompilerParams(vmem_limit_bytes=16 << 20),
        name="low_columns",
    )(parts)


def fold_rows(tall_ref, first, count):
    folded = tall_ref[pl.ds(first, count // FOLD, stride=FOLD), :]
    group = lax.broadcasted_iota(jnp.int32, folded.shape, 1) // (128 // FOLD)
    for j in range(1, FOLD):
        folded = jnp.where(group == j, tall_ref[pl.ds(first + j, count // FOLD, stride=FOLD), :], folded)
    return folded


def gradient_rows_kernel(out_ref, low_ref, wire_ref, tall_ref, wide_ref):
    _, examples, tokens, channels = out_ref.shape
    blocks = wire_ref.shape[0]
    for n in range(examples):
        factors = low_ref[n * tokens : (n + 1) * tokens, :].astype(jnp.float32)
        column = lax.rem(lax.broadcasted_iota(jnp.int32, factors.shape, 1), 128 // FOLD)
        value = column >= 64 // FOLD
        factors = jnp.concatenate([jnp.where(value, 0.0, factors), jnp.where(value, factors, 0.0)], axis=0)
        both = jnp.concatenate([out_ref[0, n], out_ref[1, n]], axis=0)
        tall_ref[...] = lax.dot_general(
            both, factors.astype(jnp.bfloat16), (((0,), (0,)), ((), ())), preferred_element_type=jnp.float32
        )
        wide_ref[pl.ds(n, channels // FOLD, stride=examples), :] = fold_rows(tall_ref, 0, channels)
    tiles = channels // FOLD // blocks
    for block in range(blocks):
        for tile in range(tiles):
            start = (block * tiles + tile) * examples
            piece = wide_ref[start : start + examples, :].astype(jnp.bfloat16)
            wire_ref[block, :, tile * 128 : (tile + 1) * 128] = piece


def gradient_rows(output_gradients, low, blocks):
    _, examples, _, channels = output_gradients.shape
    lanes = channels * 128 // FOLD // blocks
    return pl.pallas_call(
        gradient_rows_kernel,
        out_shape=jax.ShapeDtypeStruct((blocks, examples, lanes), jnp.bfloat16),
        scratch_shapes=[
            pltpu.VMEM((channels, 128), jnp.float32),
            pltpu.VMEM((channels // FOLD * examples, 128), jnp.float32),
        ],
        compiler_params=pltpu.CompilerParams(vmem_limit_bytes=16 << 20),
        name="gradient_rows",
    )(output_gradients, low)


def multiply_rows(grads_ref, rows_ref, half, held_ref, sems, acc_ref, prepare, total_ref):
    slots, group, columns, _ = held_ref.shape
    size = group * columns
    count = rows_ref.shape[0] // group

    def copy(i):
        return pltpu.make_async_copy(
            rows_ref.at[pl.ds(i * group, group), pl.ds(half * columns, columns)],
            held_ref.at[i % slots],
            sems.at[i % slots],
        )

    for i in range(min(slots, count)):
        copy(i).start()
    prepare()
    for i in range(count):
        copy(i).wait()
        product = jnp.dot(
            grads_ref[:, i * size : (i + 1) * size],
            held_ref[i % slots].reshape(size, held_ref.shape[3]),
            preferred_element_type=jnp.float32,
        )
        if i:
            acc_ref[...] += product
        elif total_ref is None:
            acc_ref[...] = product
        else:
            acc_ref[...] = total_ref[...] + product
        if i + slots < count:
            copy(i + slots).start()


def early_features_kernel(tokens_ref, low_ref, rows_ref, total_ref, grads_ref, tall_ref, wide_ref, held_ref, sems):
    examples, length, channels = tokens_ref.shape
    sources = low_ref.shape[0]
    each = examples // sources

    def prepare():
        def source(index, carry):
            factors = spread(low_ref[index].astype(jnp.float32)).astype(jnp.bfloat16)
            for n in range(each):
                tall_ref[n * channels : (n + 1) * channels, :] = lax.dot_general(
                    tokens_ref[index * each + n],
                    factors[n * length : (n + 1) * length],
                    (((0,), (0,)), ((), ())),
                    preferred_element_type=jnp.float32,
                )
            for n in range(each):
                wide_ref[pl.ds(index * each + n, channels // FOLD, stride=examples), :] = fold_rows(
                    tall_ref, n * channels, channels
                )
            return carry

        lax.fori_loop(0, sources, source, 0)
        for tile in range(channels // FOLD):
            grads_ref[:, tile * 128 : (tile + 1) * 128] = wide_ref[
                tile * examples : (tile + 1) * examples, :
            ].astype(jnp.bfloat16)

    multiply_rows(grads_ref, rows_ref, 0, held_ref, sems, total_ref, prepare, None)


def held_rows(rows):
    return [
        pltpu.VMEM((SLOTS, GROUP, rows.shape[1] // 2, rows.shape[2]), rows.dtype),
        pltpu.SemaphoreType.DMA((SLOTS,)),
    ]


def early_features(tokens, low, rows):
    examples, _, channels = tokens.shape
    in_vmem = pl.BlockSpec(memory_space=pltpu.VMEM)
    return pl.pallas_call(
        early_features_kernel,
        out_shape=jax.ShapeDtypeStruct((examples, rows.shape[2]), jnp.float32),
        in_specs=[in_vmem, in_vmem, pl.BlockSpec(memory_space=pl.ANY)],
        out_specs=in_vmem,
        scratch_shapes=[
            pltpu.VMEM((examples, channels * 128 // FOLD), jnp.bfloat16),
            pltpu.VMEM((examples // low.shape[0] * channels, 128), jnp.float32),
            pltpu.VMEM((channels // FOLD * examples, 128), jnp.float32),
        ]
        + held_rows(rows),
        compiler_params=pltpu.CompilerParams(vmem_limit_bytes=40 << 20),
        name="early_features",
    )(tokens, low, rows)


def late_features_kernel(grads_ref, rows_ref, total_ref, out_ref, acc_ref, held_ref, sems):
    multiply_rows(grads_ref, rows_ref, 1, held_ref, sems, acc_ref, lambda: None, total_ref)
    if len(out_ref.shape) == 3:
        lanes = out_ref.shape[2]
        for block in range(out_ref.shape[0]):
            out_ref[block] = acc_ref[:, block * lanes : (block + 1) * lanes].astype(out_ref.dtype)
    else:
        out_ref[...] = acc_ref[...].astype(out_ref.dtype)


def late_features(grads, rows, total, blocks):
    examples, columns = total.shape
    shape = (examples, columns) if columns // blocks % 128 else (blocks, examples, columns // blocks)
    in_vmem = pl.BlockSpec(memory_space=pltpu.VMEM)
    return pl.pallas_call(
        late_features_kernel,
        out_shape=jax.ShapeDtypeStruct(shape, jnp.bfloat16),
        in_specs=[in_vmem, pl.BlockSpec(memory_space=pl.ANY), in_vmem],
        out_specs=in_vmem,
        scratch_shapes=[pltpu.VMEM((examples, columns), jnp.float32)] + held_rows(rows),
        compiler_params=pltpu.CompilerParams(vmem_limit_bytes=40 << 20),
        name="late_features",
    )(grads, rows, total)


def packs(example_count):
    return example_count == 2 * HALF


def packed_gram_kernel(blocks_ref, row_ref, out_ref):
    features = jnp.sum(blocks_ref[...].astype(jnp.float32), axis=0)
    gram = exact_dot(features, features, ((1,), (1,)))
    upper, across, under = gram[:HALF, :HALF], gram[:HALF, HALF:], gram[HALF:, HALF:]
    rows = lax.broadcasted_iota(jnp.int32, (HALF, HALF), 0)
    cols = lax.broadcasted_iota(jnp.int32, (HALF, HALF), 1)
    mixed = jnp.where(rows <= cols, upper, under)
    quarter = HALF // 2
    body = jnp.concatenate([across[:quarter], across[quarter:], mixed[:quarter], mixed[quarter:]], axis=1)
    diagonal = jnp.sum(jnp.where(rows == cols, under, 0.0), axis=0, keepdims=True)
    last = row_ref[...] + jnp.concatenate([diagonal, jnp.zeros((1, 128 - HALF), jnp.float32)], axis=1)
    piece = jnp.concatenate([body, jnp.broadcast_to(last, (8, 128))], axis=0)
    out_ref[...] = jnp.broadcast_to(piece[None], out_ref.shape)


def packed_gram(blocks, row):
    return pl.pallas_call(
        packed_gram_kernel,
        out_shape=jax.ShapeDtypeStruct((blocks.shape[0], HALF // 2 + 8, 128), jnp.float32),
        compiler_params=pltpu.CompilerParams(vmem_limit_bytes=16 << 20),
        name="packed_gram",
    )(blocks, row)


def unpack(total):
    quarter = HALF // 2
    rows = lax.broadcasted_iota(jnp.int32, (HALF, HALF), 0)
    cols = lax.broadcasted_iota(jnp.int32, (HALF, HALF), 1)
    body = total[:quarter]
    across = jnp.concatenate([body[:, :HALF], body[:, HALF : 2 * HALF]], axis=0)
    mixed = jnp.concatenate([body[:, 2 * HALF : 3 * HALF], body[:, 3 * HALF :]], axis=0)
    turned = mixed.T
    upper = jnp.where(rows <= cols, mixed, turned)
    diagonal = jnp.broadcast_to(total[quarter : quarter + 1, :HALF], (HALF, HALF))
    under = jnp.where(rows == cols, diagonal, jnp.where(rows > cols, mixed, turned))
    gram = jnp.concatenate(
        [jnp.concatenate([upper, across], axis=1), jnp.concatenate([across.T, under], axis=1)], axis=0
    )
    return gram, total[quarter : quarter + 1, HALF : 3 * HALF]


def solve_kernel(count, slot_ref, pieces_ref, ids_ref, scores_ref, domain_ref, work_ref):
    total = jnp.sum(pieces_ref[...], axis=0)
    if packs(count):
        raw_gram, all_domains = unpack(total)
    else:
        raw_gram, all_domains = total[:count], total[count : count + 1]
    rows = lax.broadcasted_iota(jnp.int32, (count, count), 0)
    cols = lax.broadcasted_iota(jnp.int32, (count, count), 1)
    on_diagonal = jnp.where(rows == cols, raw_gram, 0.0)
    gram = raw_gram * lax.rsqrt(jnp.sum(on_diagonal, axis=1, keepdims=True) + 1e-06)
    gram = gram * lax.rsqrt(jnp.sum(on_diagonal, axis=0, keepdims=True) + 1e-06)

    work_ref[...] = gram + jnp.where(rows == cols, 0.25, 0.0)

    def sweep(k, carry):
        held = work_ref[...]
        row = work_ref[pl.ds(k, 1), :]
        pivot = 1.0 / jnp.sum(jnp.where(cols[:1] == k, row, 0.0), axis=1, keepdims=True)
        column = jnp.sum(jnp.where(cols == k, held, 0.0), axis=1, keepdims=True)
        row = jnp.where(cols[:1] == k, -pivot, row * pivot)
        column = jnp.where(rows[:, :1] == k, -1.0, column)
        work_ref[...] = jnp.where((cols == k) | (rows == k), 0.0, held) - column * row
        return carry

    lax.fori_loop(0, count, sweep, 0)

    targets = ids_ref.shape[1]
    places = lax.broadcasted_iota(jnp.int32, (count, targets), 0)
    chosen = places == ids_ref[...]
    cross = exact_dot(gram, jnp.where(chosen, 1.0, 0.0), ((1,), (0,)))
    cross = jnp.where(chosen, 0.0, cross)
    scores = exact_dot(work_ref[...], cross, ((1,), (0,))) * -math.sqrt(K)
    kinds = lax.broadcasted_iota(jnp.int32, (DOMAINS, count), 0).astype(jnp.float32)
    indicator = jnp.where(kinds == all_domains, 1.0, 0.0)
    domain_ref[...] = exact_dot(indicator, scores, ((1,), (0,))) / math.sqrt(count / DOMAINS)
    work_ref[:, :targets] = scores
    scores_ref[...] = work_ref[pl.ds(pl.multiple_of(slot_ref[0], 8), scores_ref.shape[0]), :targets]


def solve(pieces, target_ids, slot, ex_rows, count):
    targets = target_ids.shape[0]
    return pl.pallas_call(
        functools.partial(solve_kernel, count),
        out_shape=(
            jax.ShapeDtypeStruct((ex_rows, targets), jnp.float32),
            jax.ShapeDtypeStruct((DOMAINS, targets), jnp.float32),
        ),
        in_specs=[
            pl.BlockSpec(memory_space=pltpu.SMEM),
            pl.BlockSpec(memory_space=pltpu.VMEM),
            pl.BlockSpec(memory_space=pltpu.VMEM),
        ],
        out_specs=(pl.BlockSpec(memory_space=pltpu.VMEM), pl.BlockSpec(memory_space=pltpu.VMEM)),
        scratch_shapes=[pltpu.VMEM((count, count), jnp.float32)],
        compiler_params=pltpu.CompilerParams(vmem_limit_bytes=16 << 20),
        name="solve",
    )(jnp.reshape(slot, (1,)), pieces, target_ids[None])


def local(
    activations,
    output_gradients,
    down_projection_weight,
    adapter_up,
    projection,
    domains,
    target_ids,
):
    single_float = jnp.float32
    ex_rows = activations.shape[0]
    rank = down_projection_weight.shape[1]
    ex_size = lax.axis_size("ex")
    devices = lax.axis_size("param") * ex_size
    example_count = ex_rows * ex_size

    tokens = activations.shape[1]
    channels = activations.shape[2]
    owned = channels // ex_size

    wire = activations.reshape(ex_rows, tokens, ex_size, owned).transpose(2, 0, 1, 3)
    moved = swap(wire, "ex").reshape(example_count, tokens, owned)

    up_terms = jnp.einsum(
        "atd,adr->art",
        output_gradients.reshape(2, ex_rows * tokens, channels),
        adapter_up,
        preferred_element_type=single_float,
    )
    down_terms = jnp.einsum(
        "td,ard->art",
        activations.reshape(ex_rows * tokens, channels),
        down_projection_weight,
        preferred_element_type=single_float,
    )
    partial_low = jnp.concatenate([up_terms, down_terms], axis=0).reshape(4 * rank, ex_rows * tokens)
    low_parts = lax.all_gather(partial_low, "param")
    queries, rest = low_columns(low_parts, ex_size)
    queries, moved = lax.optimization_barrier((queries, moved))

    queries = swap(queries, "ex")
    grads = swap(gradient_rows(output_gradients, rest, ex_size), "ex").reshape(example_count, owned * 2 * rank)
    rows = projection.reshape(owned, 4 * rank, K)
    total = early_features(moved, queries, rows)
    partial_sums = late_features(grads, rows, total, devices)
    if partial_sums.ndim == 2:
        partial_sums = partial_sums.reshape(example_count, devices, K // devices).transpose(1, 0, 2)
    arrived = swap(partial_sums, EVERY)

    slot = lax.axis_index("ex") * ex_rows
    mine = jnp.where(lax.axis_index("param") == 0, domains, 0).astype(single_float)
    domain_row = lax.dynamic_update_slice(jnp.zeros((example_count,), single_float), mine, (slot,))
    if packs(example_count):
        row = jnp.pad(domain_row, (HALF, 128 - HALF - example_count))[None]
        pieces = swap(packed_gram(arrived, row), EVERY)
    else:
        features = jnp.sum(arrived.astype(single_float), axis=0)
        gram = exact_dot(features, features, ((1,), (1,)))
        gram = jnp.concatenate([gram, jnp.broadcast_to(domain_row, (devices, example_count))], axis=0)
        share = gram.shape[0] // devices
        summed = jnp.sum(swap(gram, EVERY).reshape(devices, share, example_count), axis=0)
        pieces = swap(jnp.broadcast_to(summed[None], (devices, share, example_count)), EVERY)
        pieces = pieces.reshape(1, devices * share, example_count)
    scores, domain_scores = solve(pieces, target_ids, slot, ex_rows, example_count)
    return (scores.T, domain_scores.T)


def solution(mesh):
    in_specs = (
        P("ex", None, "param"),
        P(None, "ex", None, "param"),
        P(None, None, "param"),
        P(None, "param", None),
        P(("param", "ex"), None),
        P("ex"),
        P("param"),
    )
    out_specs = (P("param", "ex"), P("param", None))
    return jax.shard_map(local, mesh=mesh, in_specs=in_specs, out_specs=out_specs, check_vma=False)
```

```python
import functools
import math

import jax
import jax.numpy as jnp
from jax import lax
from jax.experimental import pallas as pl
from jax.experimental.pallas import tpu as pltpu
from jax.sharding import PartitionSpec as P

K = 4096
DOMAINS = 4
HALF = 32
FOLD = 4
GROUP = 8
SLOTS = 12
EVERY = ("param", "ex")


def exact_dot(left, right, dims):
    return lax.dot_general(
        left, right, (dims, ((), ())), precision=lax.Precision.HIGHEST, preferred_element_type=jnp.float32
    )


def swap(blocks, axes):
    return lax.all_to_all(blocks, axes, split_axis=0, concat_axis=0, tiled=True)


def spread(columns):
    return jnp.concatenate([columns] * FOLD, axis=0).T


def meets(ex_size):
    return ex_size == 8


def low_columns_kernel(parts_ref, queries_ref, rest_ref):
    low = parts_ref[0]
    for part in range(1, parts_ref.shape[0]):
        low = low + parts_ref[part]
    low = low.astype(jnp.bfloat16)
    half = low.shape[0] // 2
    for block in range(queries_ref.shape[0]):
        queries_ref[block] = low[:half]
    rest_ref[...] = spread(low[half:].astype(jnp.float32)).astype(jnp.bfloat16)


def low_columns(parts, blocks):
    _, columns, tokens = parts.shape
    return pl.pallas_call(
        low_columns_kernel,
        out_shape=(
            jax.ShapeDtypeStruct((blocks, columns // 2, tokens), jnp.bfloat16),
            jax.ShapeDtypeStruct((tokens, FOLD * columns // 2), jnp.bfloat16),
        ),
        compiler_params=pltpu.CompilerParams(vmem_limit_bytes=16 << 20),
        name="low_columns",
    )(parts)


def fold_rows(tall_ref, first, count):
    folded = tall_ref[pl.ds(first, count // FOLD, stride=FOLD), :]
    group = lax.broadcasted_iota(jnp.int32, folded.shape, 1) // (128 // FOLD)
    for j in range(1, FOLD):
        folded = jnp.where(group == j, tall_ref[pl.ds(first + j, count // FOLD, stride=FOLD), :], folded)
    return folded


def gradient_rows_kernel(out_ref, low_ref, wire_ref, tall_ref, wide_ref):
    _, examples, tokens, channels = out_ref.shape
    blocks = wire_ref.shape[0]
    for n in range(examples):
        factors = low_ref[n * tokens : (n + 1) * tokens, :].astype(jnp.float32)
        column = lax.rem(lax.broadcasted_iota(jnp.int32, factors.shape, 1), 128 // FOLD)
        value = column >= 64 // FOLD
        factors = jnp.concatenate([jnp.where(value, 0.0, factors), jnp.where(value, factors, 0.0)], axis=0)
        both = jnp.concatenate([out_ref[0, n], out_ref[1, n]], axis=0)
        tall_ref[...] = lax.dot_general(
            both, factors.astype(jnp.bfloat16), (((0,), (0,)), ((), ())), preferred_element_type=jnp.float32
        )
        wide_ref[pl.ds(n, channels // FOLD, stride=examples), :] = fold_rows(tall_ref, 0, channels)
    tiles = channels // FOLD // blocks
    for block in range(blocks):
        for tile in range(tiles):
            start = (block * tiles + tile) * examples
            piece = wide_ref[start : start + examples, :].astype(jnp.bfloat16)
            wire_ref[block, :, tile * 128 : (tile + 1) * 128] = piece


def gradient_rows(output_gradients, low, blocks):
    _, examples, _, channels = output_gradients.shape
    lanes = channels * 128 // FOLD // blocks
    return pl.pallas_call(
        gradient_rows_kernel,
        out_shape=jax.ShapeDtypeStruct((blocks, examples, lanes), jnp.bfloat16),
        scratch_shapes=[
            pltpu.VMEM((channels, 128), jnp.float32),
            pltpu.VMEM((channels // FOLD * examples, 128), jnp.float32),
        ],
        compiler_params=pltpu.CompilerParams(vmem_limit_bytes=16 << 20),
        name="gradient_rows",
    )(output_gradients, low)


def multiply_rows(grads_ref, rows_ref, half, held_ref, sems, acc_ref, prepare, total_ref):
    slots, group, columns, _ = held_ref.shape
    size = group * columns
    count = rows_ref.shape[0] // group

    def copy(i):
        return pltpu.make_async_copy(
            rows_ref.at[pl.ds(i * group, group), pl.ds(half * columns, columns)],
            held_ref.at[i % slots],
            sems.at[i % slots],
        )

    for i in range(min(slots, count)):
        copy(i).start()
    prepare()
    for i in range(count):
        copy(i).wait()
        product = jnp.dot(
            grads_ref[:, i * size : (i + 1) * size],
            held_ref[i % slots].reshape(size, held_ref.shape[3]),
            preferred_element_type=jnp.float32,
        )
        if i:
            acc_ref[...] += product
        elif total_ref is None:
            acc_ref[...] = product
        else:
            acc_ref[...] = total_ref[...] + product
        if i + slots < count:
            copy(i + slots).start()


def early_features_kernel(parts, offset_ref, tokens_ref, *refs):
    rows_ref, total_ref, low_ref, grads_ref, tall_ref, wide_ref, held_ref, sems = refs[parts:]
    examples, length, channels = tokens_ref.shape
    sources = low_ref.shape[0]
    each = examples // sources

    def prepare():
        first = 0
        for part in refs[:parts]:
            low_ref[first : first + part.shape[0]] = part[...]
            first += part.shape[0]

        def source(index, carry):
            factors = spread(low_ref[lax.bitwise_xor(index, offset_ref[0])].astype(jnp.float32)).astype(jnp.bfloat16)
            for n in range(each):
                tall_ref[n * channels : (n + 1) * channels, :] = lax.dot_general(
                    tokens_ref[index * each + n],
                    factors[n * length : (n + 1) * length],
                    (((0,), (0,)), ((), ())),
                    preferred_element_type=jnp.float32,
                )
            for n in range(each):
                wide_ref[pl.ds(index * each + n, channels // FOLD, stride=examples), :] = fold_rows(
                    tall_ref, n * channels, channels
                )
            return carry

        lax.fori_loop(0, sources, source, 0)
        for tile in range(channels // FOLD):
            grads_ref[:, tile * 128 : (tile + 1) * 128] = wide_ref[
                tile * examples : (tile + 1) * examples, :
            ].astype(jnp.bfloat16)

    multiply_rows(grads_ref, rows_ref, 0, held_ref, sems, total_ref, prepare, None)


def held_rows(rows):
    return [
        pltpu.VMEM((SLOTS, GROUP, rows.shape[1] // 2, rows.shape[2]), rows.dtype),
        pltpu.SemaphoreType.DMA((SLOTS,)),
    ]


def early_features(tokens, offset, low, rows):
    examples, _, channels = tokens.shape
    sources = sum(part.shape[0] for part in low)
    in_vmem = pl.BlockSpec(memory_space=pltpu.VMEM)
    return pl.pallas_call(
        functools.partial(early_features_kernel, len(low)),
        out_shape=jax.ShapeDtypeStruct((examples, rows.shape[2]), jnp.float32),
        in_specs=[pl.BlockSpec(memory_space=pltpu.SMEM), in_vmem]
        + [in_vmem] * len(low)
        + [pl.BlockSpec(memory_space=pl.ANY)],
        out_specs=in_vmem,
        scratch_shapes=[
            pltpu.VMEM((sources, *low[0].shape[1:]), jnp.bfloat16),
            pltpu.VMEM((examples, channels * 128 // FOLD), jnp.bfloat16),
            pltpu.VMEM((examples // sources * channels, 128), jnp.float32),
            pltpu.VMEM((channels // FOLD * examples, 128), jnp.float32),
        ]
        + held_rows(rows),
        compiler_params=pltpu.CompilerParams(vmem_limit_bytes=40 << 20),
        name="early_features",
    )(jnp.reshape(offset, (1,)), tokens, *low, rows)


def late_features_kernel(grads_ref, rows_ref, total_ref, out_ref, acc_ref, held_ref, sems):
    multiply_rows(grads_ref, rows_ref, 1, held_ref, sems, acc_ref, lambda: None, total_ref)
    if len(out_ref.shape) == 3:
        lanes = out_ref.shape[2]
        for block in range(out_ref.shape[0]):
            out_ref[block] = acc_ref[:, block * lanes : (block + 1) * lanes].astype(out_ref.dtype)
    else:
        out_ref[...] = acc_ref[...].astype(out_ref.dtype)


def late_features(grads, rows, total, blocks):
    examples, columns = total.shape
    shape = (examples, columns) if columns // blocks % 128 else (blocks, examples, columns // blocks)
    in_vmem = pl.BlockSpec(memory_space=pltpu.VMEM)
    return pl.pallas_call(
        late_features_kernel,
        out_shape=jax.ShapeDtypeStruct(shape, jnp.bfloat16),
        in_specs=[in_vmem, pl.BlockSpec(memory_space=pl.ANY), in_vmem],
        out_specs=in_vmem,
        scratch_shapes=[pltpu.VMEM((examples, columns), jnp.float32)] + held_rows(rows),
        compiler_params=pltpu.CompilerParams(vmem_limit_bytes=40 << 20),
        name="late_features",
    )(grads, rows, total)


def flip(array, bits):
    return lax.ppermute(array, "ex", [(i, i ^ bits) for i in range(lax.axis_size("ex"))])


def packs(example_count):
    return example_count == 2 * HALF


def packed_gram_kernel(blocks_ref, row_ref, out_ref):
    features = jnp.sum(blocks_ref[...].astype(jnp.float32), axis=0)
    gram = exact_dot(features, features, ((1,), (1,)))
    upper, across, under = gram[:HALF, :HALF], gram[:HALF, HALF:], gram[HALF:, HALF:]
    rows = lax.broadcasted_iota(jnp.int32, (HALF, HALF), 0)
    cols = lax.broadcasted_iota(jnp.int32, (HALF, HALF), 1)
    mixed = jnp.where(rows <= cols, upper, under)
    quarter = HALF // 2
    body = jnp.concatenate([across[:quarter], across[quarter:], mixed[:quarter], mixed[quarter:]], axis=1)
    diagonal = jnp.sum(jnp.where(rows == cols, under, 0.0), axis=0, keepdims=True)
    last = row_ref[...] + jnp.concatenate([diagonal, jnp.zeros((1, 128 - HALF), jnp.float32)], axis=1)
    piece = jnp.concatenate([body, jnp.broadcast_to(last, (8, 128))], axis=0)
    out_ref[...] = jnp.broadcast_to(piece[None], out_ref.shape)


def packed_gram(blocks, row):
    return pl.pallas_call(
        packed_gram_kernel,
        out_shape=jax.ShapeDtypeStruct((blocks.shape[0], HALF // 2 + 8, 128), jnp.float32),
        compiler_params=pltpu.CompilerParams(vmem_limit_bytes=16 << 20),
        name="packed_gram",
    )(blocks, row)


def unpack(total):
    quarter = HALF // 2
    rows = lax.broadcasted_iota(jnp.int32, (HALF, HALF), 0)
    cols = lax.broadcasted_iota(jnp.int32, (HALF, HALF), 1)
    body = total[:quarter]
    across = jnp.concatenate([body[:, :HALF], body[:, HALF : 2 * HALF]], axis=0)
    mixed = jnp.concatenate([body[:, 2 * HALF : 3 * HALF], body[:, 3 * HALF :]], axis=0)
    turned = mixed.T
    upper = jnp.where(rows <= cols, mixed, turned)
    diagonal = jnp.broadcast_to(total[quarter : quarter + 1, :HALF], (HALF, HALF))
    under = jnp.where(rows == cols, diagonal, jnp.where(rows > cols, mixed, turned))
    gram = jnp.concatenate(
        [jnp.concatenate([upper, across], axis=1), jnp.concatenate([across.T, under], axis=1)], axis=0
    )
    return gram, total[quarter : quarter + 1, HALF : 3 * HALF]


def solve_kernel(count, slot_ref, pieces_ref, ids_ref, scores_ref, domain_ref, work_ref):
    total = jnp.sum(pieces_ref[...], axis=0)
    if packs(count):
        raw_gram, all_domains = unpack(total)
    else:
        raw_gram, all_domains = total[:count], total[count : count + 1]
    rows = lax.broadcasted_iota(jnp.int32, (count, count), 0)
    cols = lax.broadcasted_iota(jnp.int32, (count, count), 1)
    on_diagonal = jnp.where(rows == cols, raw_gram, 0.0)
    gram = raw_gram * lax.rsqrt(jnp.sum(on_diagonal, axis=1, keepdims=True) + 1e-06)
    gram = gram * lax.rsqrt(jnp.sum(on_diagonal, axis=0, keepdims=True) + 1e-06)

    work_ref[...] = gram + jnp.where(rows == cols, 0.25, 0.0)
    along, down = cols[:1], rows[:, :1]

    def at(array, k):
        return jnp.sum(jnp.where(along == k, array, 0.0), axis=1, keepdims=True)

    def sweep(step, carry):
        k = 2 * step
        held = work_ref[...]
        row0, row1 = work_ref[pl.ds(k, 1), :], work_ref[pl.ds(k + 1, 1), :]
        a, b, d = at(row0, k), at(row1, k), at(row1, k + 1)
        scale = 1.0 / (a * d - b * b)
        a, b, d = a * scale, b * scale, d * scale
        column0, column1 = at(held, k), at(held, k + 1)
        new0 = jnp.where(along == k, -d, jnp.where(along == k + 1, b, d * row0 - b * row1))
        new1 = jnp.where(along == k, b, jnp.where(along == k + 1, -a, a * row1 - b * row0))
        column0 = jnp.where(down == k, -1.0, jnp.where(down == k + 1, 0.0, column0))
        column1 = jnp.where(down == k, 0.0, jnp.where(down == k + 1, -1.0, column1))
        swept = (cols == k) | (cols == k + 1) | (rows == k) | (rows == k + 1)
        work_ref[...] = jnp.where(swept, 0.0, held) - column0 * new0 - column1 * new1
        return carry

    lax.fori_loop(0, count // 2, sweep, 0)

    targets = ids_ref.shape[1]
    places = lax.broadcasted_iota(jnp.int32, (count, targets), 0)
    chosen = places == ids_ref[...]
    cross = exact_dot(gram, jnp.where(chosen, 1.0, 0.0), ((1,), (0,)))
    cross = jnp.where(chosen, 0.0, cross)
    scores = exact_dot(work_ref[...], cross, ((1,), (0,))) * -math.sqrt(K)
    kinds = lax.broadcasted_iota(jnp.int32, (DOMAINS, count), 0).astype(jnp.float32)
    indicator = jnp.where(kinds == all_domains, 1.0, 0.0)
    domain_ref[...] = exact_dot(indicator, scores, ((1,), (0,))) / math.sqrt(count / DOMAINS)
    work_ref[:, :targets] = scores
    scores_ref[...] = work_ref[pl.ds(pl.multiple_of(slot_ref[0], 8), scores_ref.shape[0]), :targets]


def solve(pieces, target_ids, slot, ex_rows, count):
    targets = target_ids.shape[0]
    return pl.pallas_call(
        functools.partial(solve_kernel, count),
        out_shape=(
            jax.ShapeDtypeStruct((ex_rows, targets), jnp.float32),
            jax.ShapeDtypeStruct((DOMAINS, targets), jnp.float32),
        ),
        in_specs=[
            pl.BlockSpec(memory_space=pltpu.SMEM),
            pl.BlockSpec(memory_space=pltpu.VMEM),
            pl.BlockSpec(memory_space=pltpu.VMEM),
        ],
        out_specs=(pl.BlockSpec(memory_space=pltpu.VMEM), pl.BlockSpec(memory_space=pltpu.VMEM)),
        scratch_shapes=[pltpu.VMEM((count, count), jnp.float32)],
        compiler_params=pltpu.CompilerParams(vmem_limit_bytes=16 << 20),
        name="solve",
    )(jnp.reshape(slot, (1,)), pieces, target_ids[None])


def local(
    activations,
    output_gradients,
    down_projection_weight,
    adapter_up,
    projection,
    domains,
    target_ids,
):
    single_float = jnp.float32
    ex_rows = activations.shape[0]
    rank = down_projection_weight.shape[1]
    ex_size = lax.axis_size("ex")
    devices = lax.axis_size("param") * ex_size
    example_count = ex_rows * ex_size

    tokens = activations.shape[1]
    channels = activations.shape[2]
    owned = channels // ex_size

    wire = activations.reshape(ex_rows, tokens, ex_size, owned).transpose(2, 0, 1, 3)
    moved = swap(wire, "ex").reshape(example_count, tokens, owned)

    up_terms = jnp.einsum(
        "atd,adr->art",
        output_gradients.reshape(2, ex_rows * tokens, channels),
        adapter_up,
        preferred_element_type=single_float,
    )
    down_terms = jnp.einsum(
        "td,ard->art",
        activations.reshape(ex_rows * tokens, channels),
        down_projection_weight,
        preferred_element_type=single_float,
    )
    partial_low = jnp.concatenate([up_terms, down_terms], axis=0).reshape(4 * rank, ex_rows * tokens)
    low_parts = lax.all_gather(partial_low, "param")
    if meets(ex_size):
        queries, rest = low_columns(low_parts, 1)
        pair = jnp.concatenate([queries, flip(queries, 1)], axis=0)
        queries = [pair] + [flip(pair, bits) for bits in (2, 4, 6)]
        offset = lax.axis_index("ex")
    else:
        queries, rest = low_columns(low_parts, ex_size)
        queries, moved = lax.optimization_barrier((queries, moved))
        queries = [swap(queries, "ex")]
        offset = jnp.int32(0)

    wire = gradient_rows(output_gradients, rest, ex_size)
    queries, wire = lax.optimization_barrier((queries, wire))
    grads = swap(wire, "ex").reshape(example_count, owned * 2 * rank)
    rows = projection.reshape(owned, 4 * rank, K)
    total = early_features(moved, offset, queries, rows)
    partial_sums = late_features(grads, rows, total, devices)
    if partial_sums.ndim == 2:
        partial_sums = partial_sums.reshape(example_count, devices, K // devices).transpose(1, 0, 2)
    arrived = swap(partial_sums, EVERY)

    slot = lax.axis_index("ex") * ex_rows
    mine = jnp.where(lax.axis_index("param") == 0, domains, 0).astype(single_float)
    domain_row = lax.dynamic_update_slice(jnp.zeros((example_count,), single_float), mine, (slot,))
    if packs(example_count):
        row = jnp.pad(domain_row, (HALF, 128 - HALF - example_count))[None]
        pieces = swap(packed_gram(arrived, row), EVERY)
    else:
        features = jnp.sum(arrived.astype(single_float), axis=0)
        gram = exact_dot(features, features, ((1,), (1,)))
        gram = jnp.concatenate([gram, jnp.broadcast_to(domain_row, (devices, example_count))], axis=0)
        share = gram.shape[0] // devices
        summed = jnp.sum(swap(gram, EVERY).reshape(devices, share, example_count), axis=0)
        pieces = swap(jnp.broadcast_to(summed[None], (devices, share, example_count)), EVERY)
        pieces = pieces.reshape(1, devices * share, example_count)
    scores, domain_scores = solve(pieces, target_ids, slot, ex_rows, example_count)
    return (scores.T, domain_scores.T)


def solution(mesh):
    in_specs = (
        P("ex", None, "param"),
        P(None, "ex", None, "param"),
        P(None, None, "param"),
        P(None, "param", None),
        P(("param", "ex"), None),
        P("ex"),
        P("param"),
    )
    out_specs = (P("param", "ex"), P("param", None))
    return jax.shard_map(local, mesh=mesh, in_specs=in_specs, out_specs=out_specs, check_vma=False)
```

```python
import functools
import math

import jax
import jax.numpy as jnp
from jax import lax
from jax.experimental import pallas as pl
from jax.experimental.pallas import tpu as pltpu
from jax.sharding import PartitionSpec as P

K = 4096
DOMAINS = 4
HALF = 32
FOLD = 4
GROUP = 8
SLOTS = 12
EVERY = ("param", "ex")


def exact_dot(left, right, dims):
    return lax.dot_general(
        left, right, (dims, ((), ())), precision=lax.Precision.HIGHEST, preferred_element_type=jnp.float32
    )


def swap(blocks, axes, groups=1):
    members = None
    if groups > 1:
        members = [list(range(i, groups * blocks.shape[0], groups)) for i in range(groups)]
    return lax.all_to_all(blocks, axes, split_axis=0, concat_axis=0, axis_index_groups=members, tiled=True)


def spread(columns):
    return jnp.concatenate([columns] * FOLD, axis=0).T


def meets(ex_size):
    return ex_size == 8


def low_columns_kernel(parts_ref, queries_ref, rest_ref):
    low = parts_ref[0]
    for part in range(1, parts_ref.shape[0]):
        low = low + parts_ref[part]
    low = low.astype(jnp.bfloat16)
    half = low.shape[0] // 2
    for block in range(queries_ref.shape[0]):
        queries_ref[block] = low[:half]
    rest_ref[...] = spread(low[half:].astype(jnp.float32)).astype(jnp.bfloat16)


def low_columns(parts, blocks):
    _, columns, tokens = parts.shape
    return pl.pallas_call(
        low_columns_kernel,
        out_shape=(
            jax.ShapeDtypeStruct((blocks, columns // 2, tokens), jnp.bfloat16),
            jax.ShapeDtypeStruct((tokens, FOLD * columns // 2), jnp.bfloat16),
        ),
        compiler_params=pltpu.CompilerParams(vmem_limit_bytes=16 << 20),
        name="low_columns",
    )(parts)


def fold_rows(tall_ref, first, count):
    folded = tall_ref[pl.ds(first, count // FOLD, stride=FOLD), :]
    group = lax.broadcasted_iota(jnp.int32, folded.shape, 1) // (128 // FOLD)
    for j in range(1, FOLD):
        folded = jnp.where(group == j, tall_ref[pl.ds(first + j, count // FOLD, stride=FOLD), :], folded)
    return folded


def gradient_rows_kernel(out_ref, low_ref, wire_ref, tall_ref, wide_ref):
    _, examples, tokens, channels = out_ref.shape
    blocks = wire_ref.shape[0]
    for n in range(examples):
        factors = low_ref[n * tokens : (n + 1) * tokens, :].astype(jnp.float32)
        column = lax.rem(lax.broadcasted_iota(jnp.int32, factors.shape, 1), 128 // FOLD)
        value = column >= 64 // FOLD
        factors = jnp.concatenate([jnp.where(value, 0.0, factors), jnp.where(value, factors, 0.0)], axis=0)
        both = jnp.concatenate([out_ref[0, n], out_ref[1, n]], axis=0)
        tall_ref[...] = lax.dot_general(
            both, factors.astype(jnp.bfloat16), (((0,), (0,)), ((), ())), preferred_element_type=jnp.float32
        )
        wide_ref[pl.ds(n, channels // FOLD, stride=examples), :] = fold_rows(tall_ref, 0, channels)
    tiles = channels // FOLD // blocks
    for block in range(blocks):
        for tile in range(tiles):
            start = (block * tiles + tile) * examples
            piece = wide_ref[start : start + examples, :].astype(jnp.bfloat16)
            wire_ref[block, :, tile * 128 : (tile + 1) * 128] = piece


def gradient_rows(output_gradients, low, blocks):
    _, examples, _, channels = output_gradients.shape
    lanes = channels * 128 // FOLD // blocks
    return pl.pallas_call(
        gradient_rows_kernel,
        out_shape=jax.ShapeDtypeStruct((blocks, examples, lanes), jnp.bfloat16),
        scratch_shapes=[
            pltpu.VMEM((channels, 128), jnp.float32),
            pltpu.VMEM((channels // FOLD * examples, 128), jnp.float32),
        ],
        compiler_params=pltpu.CompilerParams(vmem_limit_bytes=16 << 20),
        name="gradient_rows",
    )(output_gradients, low)


def multiply_rows(grads_ref, rows_ref, half, held_ref, sems, acc_ref, prepare, total_ref):
    slots, group, columns, _ = held_ref.shape
    size = group * columns
    count = rows_ref.shape[0] // group

    def copy(i):
        return pltpu.make_async_copy(
            rows_ref.at[pl.ds(i * group, group), pl.ds(half * columns, columns)],
            held_ref.at[i % slots],
            sems.at[i % slots],
        )

    for i in range(min(slots, count)):
        copy(i).start()
    prepare()
    for i in range(count):
        copy(i).wait()
        product = jnp.dot(
            grads_ref[:, i * size : (i + 1) * size],
            held_ref[i % slots].reshape(size, held_ref.shape[3]),
            preferred_element_type=jnp.float32,
        )
        if i:
            acc_ref[...] += product
        elif total_ref is None:
            acc_ref[...] = product
        else:
            acc_ref[...] = total_ref[...] + product
        if i + slots < count:
            copy(i + slots).start()


def early_features_kernel(parts, offset_ref, tokens_ref, *refs):
    rows_ref, total_ref, low_ref, grads_ref, tall_ref, wide_ref, held_ref, sems = refs[parts:]
    examples, length, channels = tokens_ref.shape
    sources = low_ref.shape[0]
    each = examples // sources

    def prepare():
        first = 0
        for part in refs[:parts]:
            low_ref[first : first + part.shape[0]] = part[...]
            first += part.shape[0]

        def source(index, carry):
            factors = spread(low_ref[lax.bitwise_xor(index, offset_ref[0])].astype(jnp.float32)).astype(jnp.bfloat16)
            for n in range(each):
                tall_ref[n * channels : (n + 1) * channels, :] = lax.dot_general(
                    tokens_ref[index * each + n],
                    factors[n * length : (n + 1) * length],
                    (((0,), (0,)), ((), ())),
                    preferred_element_type=jnp.float32,
                )
            for n in range(each):
                wide_ref[pl.ds(index * each + n, channels // FOLD, stride=examples), :] = fold_rows(
                    tall_ref, n * channels, channels
                )
            return carry

        lax.fori_loop(0, sources, source, 0)
        for tile in range(channels // FOLD):
            grads_ref[:, tile * 128 : (tile + 1) * 128] = wide_ref[
                tile * examples : (tile + 1) * examples, :
            ].astype(jnp.bfloat16)

    multiply_rows(grads_ref, rows_ref, 0, held_ref, sems, total_ref, prepare, None)


def held_rows(rows):
    return [
        pltpu.VMEM((SLOTS, GROUP, rows.shape[1] // 2, rows.shape[2]), rows.dtype),
        pltpu.SemaphoreType.DMA((SLOTS,)),
    ]


def early_features(tokens, offset, low, rows):
    examples, _, channels = tokens.shape
    sources = sum(part.shape[0] for part in low)
    in_vmem = pl.BlockSpec(memory_space=pltpu.VMEM)
    return pl.pallas_call(
        functools.partial(early_features_kernel, len(low)),
        out_shape=jax.ShapeDtypeStruct((examples, rows.shape[2]), jnp.float32),
        in_specs=[pl.BlockSpec(memory_space=pltpu.SMEM), in_vmem]
        + [in_vmem] * len(low)
        + [pl.BlockSpec(memory_space=pl.ANY)],
        out_specs=in_vmem,
        scratch_shapes=[
            pltpu.VMEM((sources, *low[0].shape[1:]), jnp.bfloat16),
            pltpu.VMEM((examples, channels * 128 // FOLD), jnp.bfloat16),
            pltpu.VMEM((examples // sources * channels, 128), jnp.float32),
            pltpu.VMEM((channels // FOLD * examples, 128), jnp.float32),
        ]
        + held_rows(rows),
        compiler_params=pltpu.CompilerParams(vmem_limit_bytes=40 << 20),
        name="early_features",
    )(jnp.reshape(offset, (1,)), tokens, *low, rows)


def late_features_kernel(grads_ref, rows_ref, total_ref, out_ref, acc_ref, held_ref, sems):
    multiply_rows(grads_ref, rows_ref, 1, held_ref, sems, acc_ref, lambda: None, total_ref)
    out_ref[...] = acc_ref[...].astype(out_ref.dtype)


def late_features_paired_kernel(core_ref, grads_ref, rows_ref, total_ref, own_ref, other_ref, acc_ref, held_ref, sems):
    multiply_rows(grads_ref, rows_ref, 1, held_ref, sems, acc_ref, lambda: None, total_ref)
    pairs, _, lanes = own_ref.shape
    first = core_ref[0] == 0
    for pair in range(pairs):
        even = acc_ref[:, 2 * pair * lanes : (2 * pair + 1) * lanes]
        odd = acc_ref[:, (2 * pair + 1) * lanes : (2 * pair + 2) * lanes]
        own_ref[pair] = jnp.where(first, even, odd)
        other_ref[pair] = jnp.where(first, odd, even)


def late_features_paired(grads, rows, total, core, pairs):
    examples, columns = total.shape
    in_vmem = pl.BlockSpec(memory_space=pltpu.VMEM)
    shape = jax.ShapeDtypeStruct((pairs, examples, columns // pairs // 2), jnp.float32)
    return pl.pallas_call(
        late_features_paired_kernel,
        out_shape=(shape, shape),
        in_specs=[pl.BlockSpec(memory_space=pltpu.SMEM), in_vmem, pl.BlockSpec(memory_space=pl.ANY), in_vmem],
        out_specs=(in_vmem, in_vmem),
        scratch_shapes=[pltpu.VMEM((examples, columns), jnp.float32)] + held_rows(rows),
        compiler_params=pltpu.CompilerParams(vmem_limit_bytes=40 << 20),
        name="late_features",
    )(jnp.reshape(core, (1,)), grads, rows, total)


def late_features(grads, rows, total):
    examples, columns = total.shape
    shape = (examples, columns)
    in_vmem = pl.BlockSpec(memory_space=pltpu.VMEM)
    return pl.pallas_call(
        late_features_kernel,
        out_shape=jax.ShapeDtypeStruct(shape, jnp.bfloat16),
        in_specs=[in_vmem, pl.BlockSpec(memory_space=pl.ANY), in_vmem],
        out_specs=in_vmem,
        scratch_shapes=[pltpu.VMEM((examples, columns), jnp.float32)] + held_rows(rows),
        compiler_params=pltpu.CompilerParams(vmem_limit_bytes=40 << 20),
        name="late_features",
    )(grads, rows, total)


def flip(array, bits):
    return lax.ppermute(array, "ex", [(i, i ^ bits) for i in range(lax.axis_size("ex"))])


def packs(example_count):
    return example_count == 2 * HALF


def packed_gram_kernel(blocks_ref, row_ref, out_ref):
    features = jnp.sum(blocks_ref[...].astype(jnp.float32), axis=0)
    gram = exact_dot(features, features, ((1,), (1,)))
    upper, across, under = gram[:HALF, :HALF], gram[:HALF, HALF:], gram[HALF:, HALF:]
    rows = lax.broadcasted_iota(jnp.int32, (HALF, HALF), 0)
    cols = lax.broadcasted_iota(jnp.int32, (HALF, HALF), 1)
    mixed = jnp.where(rows <= cols, upper, under)
    quarter = HALF // 2
    body = jnp.concatenate([across[:quarter], across[quarter:], mixed[:quarter], mixed[quarter:]], axis=1)
    diagonal = jnp.sum(jnp.where(rows == cols, under, 0.0), axis=0, keepdims=True)
    last = row_ref[...] + jnp.concatenate([diagonal, jnp.zeros((1, 128 - HALF), jnp.float32)], axis=1)
    piece = jnp.concatenate([body, jnp.broadcast_to(last, (8, 128))], axis=0)
    out_ref[...] = piece


def packed_gram(blocks, row):
    return pl.pallas_call(
        packed_gram_kernel,
        out_shape=jax.ShapeDtypeStruct((HALF // 2 + 8, 128), jnp.float32),
        compiler_params=pltpu.CompilerParams(vmem_limit_bytes=16 << 20),
        name="packed_gram",
    )(blocks, row)


def unpack(total):
    quarter = HALF // 2
    rows = lax.broadcasted_iota(jnp.int32, (HALF, HALF), 0)
    cols = lax.broadcasted_iota(jnp.int32, (HALF, HALF), 1)
    body = total[:quarter]
    across = jnp.concatenate([body[:, :HALF], body[:, HALF : 2 * HALF]], axis=0)
    mixed = jnp.concatenate([body[:, 2 * HALF : 3 * HALF], body[:, 3 * HALF :]], axis=0)
    turned = mixed.T
    upper = jnp.where(rows <= cols, mixed, turned)
    diagonal = jnp.broadcast_to(total[quarter : quarter + 1, :HALF], (HALF, HALF))
    under = jnp.where(rows == cols, diagonal, jnp.where(rows > cols, mixed, turned))
    gram = jnp.concatenate(
        [jnp.concatenate([upper, across], axis=1), jnp.concatenate([across.T, under], axis=1)], axis=0
    )
    return gram, total[quarter : quarter + 1, HALF : 3 * HALF]


def solve_kernel(count, slot_ref, pieces_ref, ids_ref, scores_ref, domain_ref, work_ref):
    total = jnp.sum(pieces_ref[...], axis=0)
    if packs(count):
        raw_gram, all_domains = unpack(total)
    else:
        raw_gram, all_domains = total[:count], total[count : count + 1]
    rows = lax.broadcasted_iota(jnp.int32, (count, count), 0)
    cols = lax.broadcasted_iota(jnp.int32, (count, count), 1)
    on_diagonal = jnp.where(rows == cols, raw_gram, 0.0)
    gram = raw_gram * lax.rsqrt(jnp.sum(on_diagonal, axis=1, keepdims=True) + 1e-06)
    gram = gram * lax.rsqrt(jnp.sum(on_diagonal, axis=0, keepdims=True) + 1e-06)

    work_ref[...] = gram + jnp.where(rows == cols, 0.25, 0.0)
    along, down = cols[:1], rows[:, :1]

    def at(array, k):
        return jnp.sum(jnp.where(along == k, array, 0.0), axis=1, keepdims=True)

    def sweep(step, carry):
        k = 2 * step
        held = work_ref[...]
        row0, row1 = work_ref[pl.ds(k, 1), :], work_ref[pl.ds(k + 1, 1), :]
        a, b, d = at(row0, k), at(row1, k), at(row1, k + 1)
        scale = 1.0 / (a * d - b * b)
        a, b, d = a * scale, b * scale, d * scale
        column0, column1 = at(held, k), at(held, k + 1)
        new0 = jnp.where(along == k, -d, jnp.where(along == k + 1, b, d * row0 - b * row1))
        new1 = jnp.where(along == k, b, jnp.where(along == k + 1, -a, a * row1 - b * row0))
        column0 = jnp.where(down == k, -1.0, jnp.where(down == k + 1, 0.0, column0))
        column1 = jnp.where(down == k, 0.0, jnp.where(down == k + 1, -1.0, column1))
        swept = (cols == k) | (cols == k + 1) | (rows == k) | (rows == k + 1)
        work_ref[...] = jnp.where(swept, 0.0, held) - column0 * new0 - column1 * new1
        return carry

    lax.fori_loop(0, count // 2, sweep, 0)

    targets = ids_ref.shape[1]
    places = lax.broadcasted_iota(jnp.int32, (count, targets), 0)
    chosen = places == ids_ref[...]
    cross = exact_dot(gram, jnp.where(chosen, 1.0, 0.0), ((1,), (0,)))
    cross = jnp.where(chosen, 0.0, cross)
    scores = exact_dot(work_ref[...], cross, ((1,), (0,))) * -math.sqrt(K)
    kinds = lax.broadcasted_iota(jnp.int32, (DOMAINS, count), 0).astype(jnp.float32)
    indicator = jnp.where(kinds == all_domains, 1.0, 0.0)
    domain_ref[...] = exact_dot(indicator, scores, ((1,), (0,))) / math.sqrt(count / DOMAINS)
    work_ref[:, :targets] = scores
    scores_ref[...] = work_ref[pl.ds(pl.multiple_of(slot_ref[0], 8), scores_ref.shape[0]), :targets]


def solve(pieces, target_ids, slot, ex_rows, count):
    targets = target_ids.shape[0]
    return pl.pallas_call(
        functools.partial(solve_kernel, count),
        out_shape=(
            jax.ShapeDtypeStruct((ex_rows, targets), jnp.float32),
            jax.ShapeDtypeStruct((DOMAINS, targets), jnp.float32),
        ),
        in_specs=[
            pl.BlockSpec(memory_space=pltpu.SMEM),
            pl.BlockSpec(memory_space=pltpu.VMEM),
            pl.BlockSpec(memory_space=pltpu.VMEM),
        ],
        out_specs=(pl.BlockSpec(memory_space=pltpu.VMEM), pl.BlockSpec(memory_space=pltpu.VMEM)),
        scratch_shapes=[pltpu.VMEM((count, count), jnp.float32)],
        compiler_params=pltpu.CompilerParams(vmem_limit_bytes=16 << 20),
        name="solve",
    )(jnp.reshape(slot, (1,)), pieces, target_ids[None])


def local(
    activations,
    output_gradients,
    down_projection_weight,
    adapter_up,
    projection,
    domains,
    target_ids,
):
    single_float = jnp.float32
    ex_rows = activations.shape[0]
    rank = down_projection_weight.shape[1]
    ex_size = lax.axis_size("ex")
    devices = lax.axis_size("param") * ex_size
    example_count = ex_rows * ex_size

    tokens = activations.shape[1]
    channels = activations.shape[2]
    owned = channels // ex_size

    wire = activations.reshape(ex_rows, tokens, ex_size, owned).transpose(2, 0, 1, 3)
    moved = swap(wire, "ex").reshape(example_count, tokens, owned)

    up_terms = jnp.einsum(
        "atd,adr->art",
        output_gradients.reshape(2, ex_rows * tokens, channels),
        adapter_up,
        preferred_element_type=single_float,
    )
    down_terms = jnp.einsum(
        "td,ard->art",
        activations.reshape(ex_rows * tokens, channels),
        down_projection_weight,
        preferred_element_type=single_float,
    )
    partial_low = jnp.concatenate([up_terms, down_terms], axis=0).reshape(4 * rank, ex_rows * tokens)
    low_parts = lax.all_gather(partial_low, "param")
    if meets(ex_size):
        queries, rest = low_columns(low_parts, 1)
        pair = jnp.concatenate([queries, flip(queries, 1)], axis=0)
        queries = [pair] + [flip(pair, bits) for bits in (2, 4, 6)]
        offset = lax.axis_index("ex")
    else:
        queries, rest = low_columns(low_parts, ex_size)
        queries, moved = lax.optimization_barrier((queries, moved))
        queries = [swap(queries, "ex")]
        offset = jnp.int32(0)

    wire = gradient_rows(output_gradients, rest, ex_size)
    queries, wire = lax.optimization_barrier((queries, wire))
    grads = swap(wire, "ex").reshape(example_count, owned * 2 * rank)
    rows = projection.reshape(owned, 4 * rank, K)
    total = early_features(moved, offset, queries, rows)

    slot = lax.axis_index("ex") * ex_rows
    mine = jnp.where(lax.axis_index("param") == 0, domains, 0).astype(single_float)
    domain_row = lax.dynamic_update_slice(jnp.zeros((example_count,), single_float), mine, (slot,))
    if packs(example_count):
        row = jnp.pad(domain_row, (HALF, 128 - HALF - example_count))[None]
        core = lax.rem(lax.axis_index("ex"), 2)
        own, other = late_features_paired(grads, rows, total, core, devices // 2)
        own = (own + flip(other, 1)).astype(jnp.bfloat16)
        piece = packed_gram(swap(own, EVERY, 2), row)
        piece = piece + flip(piece, 1)
        pieces = swap(jnp.broadcast_to(piece[None], (devices // 2, *piece.shape)), EVERY, 2)
    else:
        partial_sums = late_features(grads, rows, total)
        partial_sums = partial_sums.reshape(example_count, devices, K // devices).transpose(1, 0, 2)
        arrived = swap(partial_sums, EVERY)
        features = jnp.sum(arrived.astype(single_float), axis=0)
        gram = exact_dot(features, features, ((1,), (1,)))
        gram = jnp.concatenate([gram, jnp.broadcast_to(domain_row, (devices, example_count))], axis=0)
        share = gram.shape[0] // devices
        summed = jnp.sum(swap(gram, EVERY).reshape(devices, share, example_count), axis=0)
        pieces = swap(jnp.broadcast_to(summed[None], (devices, share, example_count)), EVERY)
        pieces = pieces.reshape(1, devices * share, example_count)
    scores, domain_scores = solve(pieces, target_ids, slot, ex_rows, example_count)
    return (scores.T, domain_scores.T)


def solution(mesh):
    in_specs = (
        P("ex", None, "param"),
        P(None, "ex", None, "param"),
        P(None, None, "param"),
        P(None, "param", None),
        P(("param", "ex"), None),
        P("ex"),
        P("param"),
    )
    out_specs = (P("param", "ex"), P("param", None))
    return jax.shard_map(local, mesh=mesh, in_specs=in_specs, out_specs=out_specs, check_vma=False)
```

```python
import functools
import math

import jax
import jax.numpy as jnp
from jax import lax
from jax.experimental import pallas as pl
from jax.experimental.pallas import tpu as pltpu
from jax.sharding import PartitionSpec as P

K = 4096
DOMAINS = 4
HALF = 32
FOLD = 4
GROUP = 8
SLOTS = 12
EVERY = ("param", "ex")


def exact_dot(left, right, dims):
    return lax.dot_general(
        left, right, (dims, ((), ())), precision=lax.Precision.HIGHEST, preferred_element_type=jnp.float32
    )


def swap(blocks, axes, groups=1):
    members = None
    if groups > 1:
        members = [list(range(i, groups * blocks.shape[0], groups)) for i in range(groups)]
    return lax.all_to_all(blocks, axes, split_axis=0, concat_axis=0, axis_index_groups=members, tiled=True)


def first_sums_kernel(blocked, *refs):
    sources, low_ref, wire_ref = refs[:4], refs[4], refs[5 : 5 + blocked]
    held, sems = refs[5 + blocked : -1], refs[-1]
    copies = [pltpu.make_async_copy(source, here, sems.at[i]) for i, (source, here) in enumerate(zip(sources, held))]
    for copy in copies:
        copy.start()
    act_ref, out_ref, down_ref, up_ref = held
    examples, tokens, channels = act_ref.shape
    copies[0].wait()
    for wire in wire_ref:
        owned = wire.shape[3]
        for block in range(wire.shape[0]):
            wire[block] = act_ref[:, :, block * owned : (block + 1) * owned]
    for copy in copies[1:]:
        copy.wait()
    rank = down_ref.shape[1]
    inputs = act_ref[...].reshape(examples * tokens, channels)
    pairs = [(up_ref[i], out_ref[i].reshape(examples * tokens, channels)) for i in range(2)]
    pairs += [(down_ref[i], inputs) for i in range(2)]
    for i, (weight, values) in enumerate(pairs):
        low_ref[i * rank : (i + 1) * rank, :] = lax.dot_general(
            weight, values, (((1,), (1,)), ((), ())), preferred_element_type=jnp.float32
        )


def first_sums(activations, output_gradients, down, up, blocks):
    examples, tokens, channels = activations.shape
    out_shape = [jax.ShapeDtypeStruct((4 * down.shape[1], examples * tokens), jnp.float32)]
    if channels // blocks % 128 == 0:
        out_shape.append(jax.ShapeDtypeStruct((blocks, examples, tokens, channels // blocks), activations.dtype))
    operands = (activations, output_gradients, down, up)
    kept = [pltpu.with_memory_space_constraint(operand, pltpu.HBM) for operand in operands]
    low, *wire = pl.pallas_call(
        functools.partial(first_sums_kernel, len(out_shape) - 1),
        out_shape=out_shape,
        in_specs=[pl.BlockSpec(memory_space=pltpu.HBM)] * 4,
        scratch_shapes=[pltpu.VMEM(operand.shape, operand.dtype) for operand in operands]
        + [pltpu.SemaphoreType.DMA((4,))],
        compiler_params=pltpu.CompilerParams(vmem_limit_bytes=16 << 20),
        name="first_sums",
    )(*kept)
    return (wire[0] if wire else None), low


def spread(columns):
    return jnp.concatenate([columns] * FOLD, axis=0).T


def meets(ex_size):
    return ex_size == 8


def low_columns_kernel(parts_ref, queries_ref, rest_ref):
    low = parts_ref[0]
    for part in range(1, parts_ref.shape[0]):
        low = low + parts_ref[part]
    low = low.astype(jnp.bfloat16)
    half = low.shape[0] // 2
    for block in range(queries_ref.shape[0]):
        queries_ref[block] = low[:half]
    rest_ref[...] = spread(low[half:].astype(jnp.float32)).astype(jnp.bfloat16)


def low_columns(parts, blocks):
    _, columns, tokens = parts.shape
    return pl.pallas_call(
        low_columns_kernel,
        out_shape=(
            jax.ShapeDtypeStruct((blocks, columns // 2, tokens), jnp.bfloat16),
            jax.ShapeDtypeStruct((tokens, FOLD * columns // 2), jnp.bfloat16),
        ),
        compiler_params=pltpu.CompilerParams(vmem_limit_bytes=16 << 20),
        name="low_columns",
    )(parts)


def fold_rows(tall_ref, first, count):
    folded = tall_ref[pl.ds(first, count // FOLD, stride=FOLD), :]
    group = lax.broadcasted_iota(jnp.int32, folded.shape, 1) // (128 // FOLD)
    for j in range(1, FOLD):
        folded = jnp.where(group == j, tall_ref[pl.ds(first + j, count // FOLD, stride=FOLD), :], folded)
    return folded


def gradient_rows_kernel(out_ref, low_ref, wire_ref, tall_ref, wide_ref):
    _, examples, tokens, channels = out_ref.shape
    blocks = wire_ref.shape[0]
    for n in range(examples):
        factors = low_ref[n * tokens : (n + 1) * tokens, :].astype(jnp.float32)
        column = lax.rem(lax.broadcasted_iota(jnp.int32, factors.shape, 1), 128 // FOLD)
        value = column >= 64 // FOLD
        factors = jnp.concatenate([jnp.where(value, 0.0, factors), jnp.where(value, factors, 0.0)], axis=0)
        both = jnp.concatenate([out_ref[0, n], out_ref[1, n]], axis=0)
        tall_ref[...] = lax.dot_general(
            both, factors.astype(jnp.bfloat16), (((0,), (0,)), ((), ())), preferred_element_type=jnp.float32
        )
        wide_ref[pl.ds(n, channels // FOLD, stride=examples), :] = fold_rows(tall_ref, 0, channels)
    tiles = channels // FOLD // blocks
    for block in range(blocks):
        for tile in range(tiles):
            start = (block * tiles + tile) * examples
            piece = wide_ref[start : start + examples, :].astype(jnp.bfloat16)
            wire_ref[block, :, tile * 128 : (tile + 1) * 128] = piece


def gradient_rows(output_gradients, low, blocks):
    _, examples, _, channels = output_gradients.shape
    lanes = channels * 128 // FOLD // blocks
    return pl.pallas_call(
        gradient_rows_kernel,
        out_shape=jax.ShapeDtypeStruct((blocks, examples, lanes), jnp.bfloat16),
        scratch_shapes=[
            pltpu.VMEM((channels, 128), jnp.float32),
            pltpu.VMEM((channels // FOLD * examples, 128), jnp.float32),
        ],
        compiler_params=pltpu.CompilerParams(vmem_limit_bytes=16 << 20),
        name="gradient_rows",
    )(output_gradients, low)


def multiply_rows(grads_ref, rows_ref, half, held_ref, sems, acc_ref, prepare, total_ref):
    slots, group, columns, _ = held_ref.shape
    size = group * columns
    count = rows_ref.shape[0] // group

    def copy(i):
        return pltpu.make_async_copy(
            rows_ref.at[pl.ds(i * group, group), pl.ds(half * columns, columns)],
            held_ref.at[i % slots],
            sems.at[i % slots],
        )

    for i in range(min(slots, count)):
        copy(i).start()
    prepare()
    for i in range(count):
        copy(i).wait()
        product = jnp.dot(
            grads_ref[:, i * size : (i + 1) * size],
            held_ref[i % slots].reshape(size, held_ref.shape[3]),
            preferred_element_type=jnp.float32,
        )
        if i:
            acc_ref[...] += product
        elif total_ref is None:
            acc_ref[...] = product
        else:
            acc_ref[...] = total_ref[...] + product
        if i + slots < count:
            copy(i + slots).start()


def early_features_kernel(parts, offset_ref, tokens_ref, *refs):
    rows_ref, total_ref, low_ref, grads_ref, tall_ref, wide_ref, held_ref, sems = refs[parts:]
    examples, length, channels = tokens_ref.shape
    sources = low_ref.shape[0]
    each = examples // sources

    def prepare():
        first = 0
        for part in refs[:parts]:
            low_ref[first : first + part.shape[0]] = part[...]
            first += part.shape[0]

        def source(index, carry):
            factors = spread(low_ref[lax.bitwise_xor(index, offset_ref[0])].astype(jnp.float32)).astype(jnp.bfloat16)
            for n in range(each):
                tall_ref[n * channels : (n + 1) * channels, :] = lax.dot_general(
                    tokens_ref[index * each + n],
                    factors[n * length : (n + 1) * length],
                    (((0,), (0,)), ((), ())),
                    preferred_element_type=jnp.float32,
                )
            for n in range(each):
                wide_ref[pl.ds(index * each + n, channels // FOLD, stride=examples), :] = fold_rows(
                    tall_ref, n * channels, channels
                )
            return carry

        lax.fori_loop(0, sources, source, 0)
        for tile in range(channels // FOLD):
            grads_ref[:, tile * 128 : (tile + 1) * 128] = wide_ref[
                tile * examples : (tile + 1) * examples, :
            ].astype(jnp.bfloat16)

    multiply_rows(grads_ref, rows_ref, 0, held_ref, sems, total_ref, prepare, None)


def held_rows(rows):
    return [
        pltpu.VMEM((SLOTS, GROUP, rows.shape[1] // 2, rows.shape[2]), rows.dtype),
        pltpu.SemaphoreType.DMA((SLOTS,)),
    ]


def early_features(tokens, offset, low, rows):
    examples, _, channels = tokens.shape
    sources = sum(part.shape[0] for part in low)
    in_vmem = pl.BlockSpec(memory_space=pltpu.VMEM)
    return pl.pallas_call(
        functools.partial(early_features_kernel, len(low)),
        out_shape=jax.ShapeDtypeStruct((examples, rows.shape[2]), jnp.float32),
        in_specs=[pl.BlockSpec(memory_space=pltpu.SMEM), in_vmem]
        + [in_vmem] * len(low)
        + [pl.BlockSpec(memory_space=pl.ANY)],
        out_specs=in_vmem,
        scratch_shapes=[
            pltpu.VMEM((sources, *low[0].shape[1:]), jnp.bfloat16),
            pltpu.VMEM((examples, channels * 128 // FOLD), jnp.bfloat16),
            pltpu.VMEM((examples // sources * channels, 128), jnp.float32),
            pltpu.VMEM((channels // FOLD * examples, 128), jnp.float32),
        ]
        + held_rows(rows),
        compiler_params=pltpu.CompilerParams(vmem_limit_bytes=40 << 20),
        name="early_features",
    )(jnp.reshape(offset, (1,)), tokens, *low, rows)


def late_features_kernel(grads_ref, rows_ref, total_ref, out_ref, acc_ref, held_ref, sems):
    multiply_rows(grads_ref, rows_ref, 1, held_ref, sems, acc_ref, lambda: None, total_ref)
    out_ref[...] = acc_ref[...].astype(out_ref.dtype)


def late_features_paired_kernel(core_ref, grads_ref, rows_ref, total_ref, own_ref, other_ref, acc_ref, held_ref, sems):
    multiply_rows(grads_ref, rows_ref, 1, held_ref, sems, acc_ref, lambda: None, total_ref)
    pairs, _, lanes = own_ref.shape
    first = core_ref[0] == 0
    for pair in range(pairs):
        even = acc_ref[:, 2 * pair * lanes : (2 * pair + 1) * lanes]
        odd = acc_ref[:, (2 * pair + 1) * lanes : (2 * pair + 2) * lanes]
        own_ref[pair] = jnp.where(first, even, odd)
        other_ref[pair] = jnp.where(first, odd, even)


def late_features_paired(grads, rows, total, core, pairs):
    examples, columns = total.shape
    in_vmem = pl.BlockSpec(memory_space=pltpu.VMEM)
    shape = jax.ShapeDtypeStruct((pairs, examples, columns // pairs // 2), jnp.float32)
    return pl.pallas_call(
        late_features_paired_kernel,
        out_shape=(shape, shape),
        in_specs=[pl.BlockSpec(memory_space=pltpu.SMEM), in_vmem, pl.BlockSpec(memory_space=pl.ANY), in_vmem],
        out_specs=(in_vmem, in_vmem),
        scratch_shapes=[pltpu.VMEM((examples, columns), jnp.float32)] + held_rows(rows),
        compiler_params=pltpu.CompilerParams(vmem_limit_bytes=40 << 20),
        name="late_features",
    )(jnp.reshape(core, (1,)), grads, rows, total)


def late_features(grads, rows, total):
    examples, columns = total.shape
    shape = (examples, columns)
    in_vmem = pl.BlockSpec(memory_space=pltpu.VMEM)
    return pl.pallas_call(
        late_features_kernel,
        out_shape=jax.ShapeDtypeStruct(shape, jnp.bfloat16),
        in_specs=[in_vmem, pl.BlockSpec(memory_space=pl.ANY), in_vmem],
        out_specs=in_vmem,
        scratch_shapes=[pltpu.VMEM((examples, columns), jnp.float32)] + held_rows(rows),
        compiler_params=pltpu.CompilerParams(vmem_limit_bytes=40 << 20),
        name="late_features",
    )(grads, rows, total)


def flip(array, bits):
    return lax.ppermute(array, "ex", [(i, i ^ bits) for i in range(lax.axis_size("ex"))])


def packs(example_count):
    return example_count == 2 * HALF


def packed_gram_kernel(blocks_ref, row_ref, out_ref):
    features = jnp.sum(blocks_ref[...].astype(jnp.float32), axis=0)
    gram = exact_dot(features, features, ((1,), (1,)))
    upper, across, under = gram[:HALF, :HALF], gram[:HALF, HALF:], gram[HALF:, HALF:]
    rows = lax.broadcasted_iota(jnp.int32, (HALF, HALF), 0)
    cols = lax.broadcasted_iota(jnp.int32, (HALF, HALF), 1)
    mixed = jnp.where(rows <= cols, upper, under)
    quarter = HALF // 2
    body = jnp.concatenate([across[:quarter], across[quarter:], mixed[:quarter], mixed[quarter:]], axis=1)
    diagonal = jnp.sum(jnp.where(rows == cols, under, 0.0), axis=0, keepdims=True)
    last = row_ref[...] + jnp.concatenate([diagonal, jnp.zeros((1, 128 - HALF), jnp.float32)], axis=1)
    piece = jnp.concatenate([body, jnp.broadcast_to(last, (8, 128))], axis=0)
    out_ref[...] = piece


def packed_gram(blocks, row):
    return pl.pallas_call(
        packed_gram_kernel,
        out_shape=jax.ShapeDtypeStruct((HALF // 2 + 8, 128), jnp.float32),
        compiler_params=pltpu.CompilerParams(vmem_limit_bytes=16 << 20),
        name="packed_gram",
    )(blocks, row)


def unpack(total):
    quarter = HALF // 2
    rows = lax.broadcasted_iota(jnp.int32, (HALF, HALF), 0)
    cols = lax.broadcasted_iota(jnp.int32, (HALF, HALF), 1)
    body = total[:quarter]
    across = jnp.concatenate([body[:, :HALF], body[:, HALF : 2 * HALF]], axis=0)
    mixed = jnp.concatenate([body[:, 2 * HALF : 3 * HALF], body[:, 3 * HALF :]], axis=0)
    turned = mixed.T
    upper = jnp.where(rows <= cols, mixed, turned)
    diagonal = jnp.broadcast_to(total[quarter : quarter + 1, :HALF], (HALF, HALF))
    under = jnp.where(rows == cols, diagonal, jnp.where(rows > cols, mixed, turned))
    gram = jnp.concatenate(
        [jnp.concatenate([upper, across], axis=1), jnp.concatenate([across.T, under], axis=1)], axis=0
    )
    return gram, total[quarter : quarter + 1, HALF : 3 * HALF]


def solve_kernel(count, slot_ref, pieces_ref, ids_ref, scores_ref, domain_ref, work_ref):
    total = jnp.sum(pieces_ref[...], axis=0)
    if packs(count):
        raw_gram, all_domains = unpack(total)
    else:
        raw_gram, all_domains = total[:count], total[count : count + 1]
    rows = lax.broadcasted_iota(jnp.int32, (count, count), 0)
    cols = lax.broadcasted_iota(jnp.int32, (count, count), 1)
    on_diagonal = jnp.where(rows == cols, raw_gram, 0.0)
    gram = raw_gram * lax.rsqrt(jnp.sum(on_diagonal, axis=1, keepdims=True) + 1e-06)
    gram = gram * lax.rsqrt(jnp.sum(on_diagonal, axis=0, keepdims=True) + 1e-06)

    work_ref[...] = gram + jnp.where(rows == cols, 0.25, 0.0)
    along, down = cols[:1], rows[:, :1]

    def at(array, k):
        return jnp.sum(jnp.where(along == k, array, 0.0), axis=1, keepdims=True)

    def sweep(step, carry):
        k = 2 * step
        held = work_ref[...]
        row0, row1 = work_ref[pl.ds(k, 1), :], work_ref[pl.ds(k + 1, 1), :]
        a, b, d = at(row0, k), at(row1, k), at(row1, k + 1)
        scale = 1.0 / (a * d - b * b)
        a, b, d = a * scale, b * scale, d * scale
        column0, column1 = at(held, k), at(held, k + 1)
        new0 = jnp.where(along == k, -d, jnp.where(along == k + 1, b, d * row0 - b * row1))
        new1 = jnp.where(along == k, b, jnp.where(along == k + 1, -a, a * row1 - b * row0))
        column0 = jnp.where(down == k, -1.0, jnp.where(down == k + 1, 0.0, column0))
        column1 = jnp.where(down == k, 0.0, jnp.where(down == k + 1, -1.0, column1))
        swept = (cols == k) | (cols == k + 1) | (rows == k) | (rows == k + 1)
        work_ref[...] = jnp.where(swept, 0.0, held) - column0 * new0 - column1 * new1
        return carry

    lax.fori_loop(0, count // 2, sweep, 0)

    targets = ids_ref.shape[1]
    places = lax.broadcasted_iota(jnp.int32, (count, targets), 0)
    chosen = places == ids_ref[...]
    cross = exact_dot(gram, jnp.where(chosen, 1.0, 0.0), ((1,), (0,)))
    cross = jnp.where(chosen, 0.0, cross)
    scores = exact_dot(work_ref[...], cross, ((1,), (0,))) * -math.sqrt(K)
    kinds = lax.broadcasted_iota(jnp.int32, (DOMAINS, count), 0).astype(jnp.float32)
    indicator = jnp.where(kinds == all_domains, 1.0, 0.0)
    domain_ref[...] = exact_dot(indicator, scores, ((1,), (0,))) / math.sqrt(count / DOMAINS)
    work_ref[:, :targets] = scores
    scores_ref[...] = work_ref[pl.ds(pl.multiple_of(slot_ref[0], 8), scores_ref.shape[0]), :targets]


def solve(pieces, target_ids, slot, ex_rows, count):
    targets = target_ids.shape[0]
    return pl.pallas_call(
        functools.partial(solve_kernel, count),
        out_shape=(
            jax.ShapeDtypeStruct((ex_rows, targets), jnp.float32),
            jax.ShapeDtypeStruct((DOMAINS, targets), jnp.float32),
        ),
        in_specs=[
            pl.BlockSpec(memory_space=pltpu.SMEM),
            pl.BlockSpec(memory_space=pltpu.VMEM),
            pl.BlockSpec(memory_space=pltpu.VMEM),
        ],
        out_specs=(pl.BlockSpec(memory_space=pltpu.VMEM), pl.BlockSpec(memory_space=pltpu.VMEM)),
        scratch_shapes=[pltpu.VMEM((count, count), jnp.float32)],
        compiler_params=pltpu.CompilerParams(vmem_limit_bytes=16 << 20),
        name="solve",
    )(jnp.reshape(slot, (1,)), pieces, target_ids[None])


def local(
    activations,
    output_gradients,
    down_projection_weight,
    adapter_up,
    projection,
    domains,
    target_ids,
):
    single_float = jnp.float32
    ex_rows = activations.shape[0]
    rank = down_projection_weight.shape[1]
    ex_size = lax.axis_size("ex")
    devices = lax.axis_size("param") * ex_size
    example_count = ex_rows * ex_size

    tokens = activations.shape[1]
    channels = activations.shape[2]
    owned = channels // ex_size

    wire, partial_low = first_sums(
        activations, output_gradients, down_projection_weight, adapter_up.swapaxes(1, 2), ex_size
    )
    if wire is None:
        wire = activations.reshape(ex_rows, tokens, ex_size, owned).transpose(2, 0, 1, 3)
    moved = swap(wire, "ex").reshape(example_count, tokens, owned)

    low_parts = lax.all_gather(partial_low, "param")
    if meets(ex_size):
        queries, rest = low_columns(low_parts, 1)
        pair = jnp.concatenate([queries, flip(queries, 1)], axis=0)
        queries = [pair] + [flip(pair, bits) for bits in (2, 4, 6)]
        offset = lax.axis_index("ex")
    else:
        queries, rest = low_columns(low_parts, ex_size)
        queries, moved = lax.optimization_barrier((queries, moved))
        queries = [swap(queries, "ex")]
        offset = jnp.int32(0)

    wire = gradient_rows(output_gradients, rest, ex_size)
    queries, wire = lax.optimization_barrier((queries, wire))
    grads = swap(wire, "ex").reshape(example_count, owned * 2 * rank)
    rows = projection.reshape(owned, 4 * rank, K)
    total = early_features(moved, offset, queries, rows)

    slot = lax.axis_index("ex") * ex_rows
    mine = jnp.where(lax.axis_index("param") == 0, domains, 0).astype(single_float)
    domain_row = lax.dynamic_update_slice(jnp.zeros((example_count,), single_float), mine, (slot,))
    if packs(example_count):
        row = jnp.pad(domain_row, (HALF, 128 - HALF - example_count))[None]
        core = lax.rem(lax.axis_index("ex"), 2)
        own, other = late_features_paired(grads, rows, total, core, devices // 2)
        own = (own + flip(other, 1)).astype(jnp.bfloat16)
        piece = packed_gram(swap(own, EVERY, 2), row)
        piece = piece + flip(piece, 1)
        pieces = swap(jnp.broadcast_to(piece[None], (devices // 2, *piece.shape)), EVERY, 2)
    else:
        partial_sums = late_features(grads, rows, total)
        partial_sums = partial_sums.reshape(example_count, devices, K // devices).transpose(1, 0, 2)
        arrived = swap(partial_sums, EVERY)
        features = jnp.sum(arrived.astype(single_float), axis=0)
        gram = exact_dot(features, features, ((1,), (1,)))
        gram = jnp.concatenate([gram, jnp.broadcast_to(domain_row, (devices, example_count))], axis=0)
        share = gram.shape[0] // devices
        summed = jnp.sum(swap(gram, EVERY).reshape(devices, share, example_count), axis=0)
        pieces = swap(jnp.broadcast_to(summed[None], (devices, share, example_count)), EVERY)
        pieces = pieces.reshape(1, devices * share, example_count)
    scores, domain_scores = solve(pieces, target_ids, slot, ex_rows, example_count)
    return (scores.T, domain_scores.T)


def solution(mesh):
    in_specs = (
        P("ex", None, "param"),
        P(None, "ex", None, "param"),
        P(None, None, "param"),
        P(None, "param", None),
        P(("param", "ex"), None),
        P("ex"),
        P("param"),
    )
    out_specs = (P("param", "ex"), P("param", None))
    return jax.shard_map(local, mesh=mesh, in_specs=in_specs, out_specs=out_specs, check_vma=False)
```

```python
import functools
import math

import jax
import jax.numpy as jnp
from jax import lax
from jax.experimental import pallas as pl
from jax.experimental.pallas import tpu as pltpu
from jax.sharding import PartitionSpec as P

K = 4096
DOMAINS = 4
HALF = 32
FOLD = 4
GROUP = 8
SLOTS = 12
EVERY = ("param", "ex")


def exact_dot(left, right, dims):
    return lax.dot_general(
        left, right, (dims, ((), ())), precision=lax.Precision.HIGHEST, preferred_element_type=jnp.float32
    )


def swap(blocks, axes, groups=1):
    members = None
    if groups > 1:
        members = [list(range(i, groups * blocks.shape[0], groups)) for i in range(groups)]
    return lax.all_to_all(blocks, axes, split_axis=0, concat_axis=0, axis_index_groups=members, tiled=True)


def first_sums_kernel(blocked, *refs):
    sources, low_ref, wire_ref = refs[:4], refs[4], refs[5 : 5 + blocked]
    held, sems = refs[5 + blocked : -1], refs[-1]
    copies = [pltpu.make_async_copy(source, here, sems.at[i]) for i, (source, here) in enumerate(zip(sources, held))]
    for copy in copies:
        copy.start()
    act_ref, out_ref, down_ref, up_ref = held
    examples, tokens, channels = act_ref.shape
    copies[0].wait()
    for wire in wire_ref:
        owned = wire.shape[3]
        for block in range(wire.shape[0]):
            wire[block] = act_ref[:, :, block * owned : (block + 1) * owned]
    for copy in copies[1:]:
        copy.wait()
    rank = down_ref.shape[1]
    inputs = act_ref[...].reshape(examples * tokens, channels)
    pairs = [(up_ref[i], out_ref[i].reshape(examples * tokens, channels)) for i in range(2)]
    pairs += [(down_ref[i], inputs) for i in range(2)]
    for i, (weight, values) in enumerate(pairs):
        low_ref[i * rank : (i + 1) * rank, :] = lax.dot_general(
            weight, values, (((1,), (1,)), ((), ())), preferred_element_type=jnp.float32
        )


def first_sums(activations, output_gradients, down, up, blocks):
    examples, tokens, channels = activations.shape
    out_shape = [jax.ShapeDtypeStruct((4 * down.shape[1], examples * tokens), jnp.float32)]
    if channels // blocks % 128 == 0:
        out_shape.append(jax.ShapeDtypeStruct((blocks, examples, tokens, channels // blocks), activations.dtype))
    operands = (activations, output_gradients, down, up)
    kept = [pltpu.with_memory_space_constraint(operand, pltpu.HBM) for operand in operands]
    low, *wire = pl.pallas_call(
        functools.partial(first_sums_kernel, len(out_shape) - 1),
        out_shape=out_shape,
        in_specs=[pl.BlockSpec(memory_space=pltpu.HBM)] * 4,
        scratch_shapes=[pltpu.VMEM(operand.shape, operand.dtype) for operand in operands]
        + [pltpu.SemaphoreType.DMA((4,))],
        compiler_params=pltpu.CompilerParams(vmem_limit_bytes=16 << 20),
        name="first_sums",
    )(*kept)
    return (wire[0] if wire else None), low


def spread(columns):
    return jnp.concatenate([columns] * FOLD, axis=0).T


def meets(ex_size):
    return ex_size == 8


def low_columns_kernel(parts_ref, queries_ref, rest_ref):
    low = parts_ref[0]
    for part in range(1, parts_ref.shape[0]):
        low = low + parts_ref[part]
    low = low.astype(jnp.bfloat16)
    half = low.shape[0] // 2
    for block in range(queries_ref.shape[0]):
        queries_ref[block] = low[:half]
    rest_ref[...] = spread(low[half:].astype(jnp.float32)).astype(jnp.bfloat16)


def low_columns(parts, blocks):
    _, columns, tokens = parts.shape
    return pl.pallas_call(
        low_columns_kernel,
        out_shape=(
            jax.ShapeDtypeStruct((blocks, columns // 2, tokens), jnp.bfloat16),
            jax.ShapeDtypeStruct((tokens, FOLD * columns // 2), jnp.bfloat16),
        ),
        compiler_params=pltpu.CompilerParams(vmem_limit_bytes=16 << 20),
        name="low_columns",
    )(parts)


def fold_rows(tall_ref, first, count):
    folded = tall_ref[pl.ds(first, count // FOLD, stride=FOLD), :]
    group = lax.broadcasted_iota(jnp.int32, folded.shape, 1) // (128 // FOLD)
    for j in range(1, FOLD):
        folded = jnp.where(group == j, tall_ref[pl.ds(first + j, count // FOLD, stride=FOLD), :], folded)
    return folded


def gradient_rows_kernel(out_ref, low_ref, wire_ref, tall_ref, wide_ref):
    _, examples, tokens, channels = out_ref.shape
    blocks = wire_ref.shape[0]
    for n in range(examples):
        factors = low_ref[n * tokens : (n + 1) * tokens, :].astype(jnp.float32)
        column = lax.rem(lax.broadcasted_iota(jnp.int32, factors.shape, 1), 128 // FOLD)
        value = column >= 64 // FOLD
        factors = jnp.concatenate([jnp.where(value, 0.0, factors), jnp.where(value, factors, 0.0)], axis=0)
        both = jnp.concatenate([out_ref[0, n], out_ref[1, n]], axis=0)
        tall_ref[...] = lax.dot_general(
            both, factors.astype(jnp.bfloat16), (((0,), (0,)), ((), ())), preferred_element_type=jnp.float32
        )
        wide_ref[pl.ds(n, channels // FOLD, stride=examples), :] = fold_rows(tall_ref, 0, channels)
    tiles = channels // FOLD // blocks
    for block in range(blocks):
        for tile in range(tiles):
            start = (block * tiles + tile) * examples
            piece = wide_ref[start : start + examples, :].astype(jnp.bfloat16)
            wire_ref[block, :, tile * 128 : (tile + 1) * 128] = piece


def gradient_rows(output_gradients, low, blocks):
    _, examples, _, channels = output_gradients.shape
    lanes = channels * 128 // FOLD // blocks
    return pl.pallas_call(
        gradient_rows_kernel,
        out_shape=jax.ShapeDtypeStruct((blocks, examples, lanes), jnp.bfloat16),
        scratch_shapes=[
            pltpu.VMEM((channels, 128), jnp.float32),
            pltpu.VMEM((channels // FOLD * examples, 128), jnp.float32),
        ],
        compiler_params=pltpu.CompilerParams(vmem_limit_bytes=16 << 20),
        name="gradient_rows",
    )(output_gradients, low)


def multiply_rows(grads_ref, rows_ref, half, held_ref, sems, acc_ref, prepare, total_ref):
    slots, group, columns, _ = held_ref.shape
    size = group * columns
    count = rows_ref.shape[0] // group

    def copy(i):
        return pltpu.make_async_copy(
            rows_ref.at[pl.ds(i * group, group), pl.ds(half * columns, columns)],
            held_ref.at[i % slots],
            sems.at[i % slots],
        )

    for i in range(min(slots, count)):
        copy(i).start()
    prepare()
    for i in range(count):
        copy(i).wait()
        product = jnp.dot(
            grads_ref[:, i * size : (i + 1) * size],
            held_ref[i % slots].reshape(size, held_ref.shape[3]),
            preferred_element_type=jnp.float32,
        )
        if i:
            acc_ref[...] += product
        elif total_ref is None:
            acc_ref[...] = product
        else:
            acc_ref[...] = total_ref[...] + product
        if i + slots < count:
            copy(i + slots).start()


def early_features_kernel(parts, offset_ref, tokens_ref, *refs):
    rows_ref, total_ref, low_ref, grads_ref, tall_ref, wide_ref, held_ref, sems = refs[parts:]
    examples, length, channels = tokens_ref.shape
    sources = low_ref.shape[0]
    each = examples // sources

    def prepare():
        first = 0
        for part in refs[:parts]:
            low_ref[first : first + part.shape[0]] = part[...]
            first += part.shape[0]

        def source(index, carry):
            factors = spread(low_ref[lax.bitwise_xor(index, offset_ref[0])].astype(jnp.float32)).astype(jnp.bfloat16)
            for n in range(each):
                tall_ref[n * channels : (n + 1) * channels, :] = lax.dot_general(
                    tokens_ref[index * each + n],
                    factors[n * length : (n + 1) * length],
                    (((0,), (0,)), ((), ())),
                    preferred_element_type=jnp.float32,
                )
            for n in range(each):
                wide_ref[pl.ds(index * each + n, channels // FOLD, stride=examples), :] = fold_rows(
                    tall_ref, n * channels, channels
                )
            return carry

        lax.fori_loop(0, sources, source, 0)
        for tile in range(channels // FOLD):
            grads_ref[:, tile * 128 : (tile + 1) * 128] = wide_ref[
                tile * examples : (tile + 1) * examples, :
            ].astype(jnp.bfloat16)

    multiply_rows(grads_ref, rows_ref, 0, held_ref, sems, total_ref, prepare, None)


def held_rows(rows):
    return [
        pltpu.VMEM((SLOTS, GROUP, rows.shape[1] // 2, rows.shape[2]), rows.dtype),
        pltpu.SemaphoreType.DMA((SLOTS,)),
    ]


def early_features(tokens, offset, low, rows):
    examples, _, channels = tokens.shape
    sources = sum(part.shape[0] for part in low)
    in_vmem = pl.BlockSpec(memory_space=pltpu.VMEM)
    return pl.pallas_call(
        functools.partial(early_features_kernel, len(low)),
        out_shape=jax.ShapeDtypeStruct((examples, rows.shape[2]), jnp.float32),
        in_specs=[pl.BlockSpec(memory_space=pltpu.SMEM), in_vmem]
        + [in_vmem] * len(low)
        + [pl.BlockSpec(memory_space=pl.ANY)],
        out_specs=in_vmem,
        scratch_shapes=[
            pltpu.VMEM((sources, *low[0].shape[1:]), jnp.bfloat16),
            pltpu.VMEM((examples, channels * 128 // FOLD), jnp.bfloat16),
            pltpu.VMEM((examples // sources * channels, 128), jnp.float32),
            pltpu.VMEM((channels // FOLD * examples, 128), jnp.float32),
        ]
        + held_rows(rows),
        compiler_params=pltpu.CompilerParams(vmem_limit_bytes=40 << 20),
        name="early_features",
    )(jnp.reshape(offset, (1,)), tokens, *low, rows)


def late_features_kernel(grads_ref, rows_ref, total_ref, out_ref, acc_ref, held_ref, sems):
    multiply_rows(grads_ref, rows_ref, 1, held_ref, sems, acc_ref, lambda: None, total_ref)
    out_ref[...] = acc_ref[...].astype(out_ref.dtype)


def late_features_paired_kernel(core_ref, grads_ref, rows_ref, total_ref, own_ref, other_ref, acc_ref, held_ref, sems):
    multiply_rows(grads_ref, rows_ref, 1, held_ref, sems, acc_ref, lambda: None, total_ref)
    pairs, _, lanes = own_ref.shape
    first = core_ref[0] == 0
    for pair in range(pairs):
        even = acc_ref[:, 2 * pair * lanes : (2 * pair + 1) * lanes]
        odd = acc_ref[:, (2 * pair + 1) * lanes : (2 * pair + 2) * lanes]
        own_ref[pair] = jnp.where(first, even, odd)
        other_ref[pair] = jnp.where(first, odd, even)


def late_features_paired(grads, rows, total, core, pairs):
    examples, columns = total.shape
    in_vmem = pl.BlockSpec(memory_space=pltpu.VMEM)
    shape = jax.ShapeDtypeStruct((pairs, examples, columns // pairs // 2), jnp.float32)
    return pl.pallas_call(
        late_features_paired_kernel,
        out_shape=(shape, shape),
        in_specs=[pl.BlockSpec(memory_space=pltpu.SMEM), in_vmem, pl.BlockSpec(memory_space=pl.ANY), in_vmem],
        out_specs=(in_vmem, in_vmem),
        scratch_shapes=[pltpu.VMEM((examples, columns), jnp.float32)] + held_rows(rows),
        compiler_params=pltpu.CompilerParams(vmem_limit_bytes=40 << 20),
        name="late_features",
    )(jnp.reshape(core, (1,)), grads, rows, total)


def late_features(grads, rows, total):
    examples, columns = total.shape
    shape = (examples, columns)
    in_vmem = pl.BlockSpec(memory_space=pltpu.VMEM)
    return pl.pallas_call(
        late_features_kernel,
        out_shape=jax.ShapeDtypeStruct(shape, jnp.bfloat16),
        in_specs=[in_vmem, pl.BlockSpec(memory_space=pl.ANY), in_vmem],
        out_specs=in_vmem,
        scratch_shapes=[pltpu.VMEM((examples, columns), jnp.float32)] + held_rows(rows),
        compiler_params=pltpu.CompilerParams(vmem_limit_bytes=40 << 20),
        name="late_features",
    )(grads, rows, total)


def flip(array, bits):
    return lax.ppermute(array, "ex", [(i, i ^ bits) for i in range(lax.axis_size("ex"))])


def packs(example_count):
    return example_count == 2 * HALF


def packed_gram_kernel(blocks_ref, row_ref, out_ref):
    features = jnp.sum(blocks_ref[...].astype(jnp.float32), axis=0)
    gram = exact_dot(features, features, ((1,), (1,)))
    upper, across, under = gram[:HALF, :HALF], gram[:HALF, HALF:], gram[HALF:, HALF:]
    rows = lax.broadcasted_iota(jnp.int32, (HALF, HALF), 0)
    cols = lax.broadcasted_iota(jnp.int32, (HALF, HALF), 1)
    mixed = jnp.where(rows <= cols, upper, under)
    quarter = HALF // 2
    body = jnp.concatenate([across[:quarter], across[quarter:], mixed[:quarter], mixed[quarter:]], axis=1)
    diagonal = jnp.sum(jnp.where(rows == cols, under, 0.0), axis=0, keepdims=True)
    last = row_ref[...] + jnp.concatenate([diagonal, jnp.zeros((1, 128 - HALF), jnp.float32)], axis=1)
    for i in range(quarter):
        out_ref[:, i * 128 : (i + 1) * 128] = body[i : i + 1]
    out_ref[:, quarter * 128 :] = last


def packed_gram(blocks, row):
    return pl.pallas_call(
        packed_gram_kernel,
        out_shape=jax.ShapeDtypeStruct((1, (HALF // 2 + 1) * 128), jnp.float32),
        compiler_params=pltpu.CompilerParams(vmem_limit_bytes=16 << 20),
        name="packed_gram",
    )(blocks, row)


def unpack(total):
    quarter = HALF // 2
    rows = lax.broadcasted_iota(jnp.int32, (HALF, HALF), 0)
    cols = lax.broadcasted_iota(jnp.int32, (HALF, HALF), 1)
    body = total[:quarter]
    across = jnp.concatenate([body[:, :HALF], body[:, HALF : 2 * HALF]], axis=0)
    mixed = jnp.concatenate([body[:, 2 * HALF : 3 * HALF], body[:, 3 * HALF :]], axis=0)
    turned = mixed.T
    upper = jnp.where(rows <= cols, mixed, turned)
    diagonal = jnp.broadcast_to(total[quarter : quarter + 1, :HALF], (HALF, HALF))
    under = jnp.where(rows == cols, diagonal, jnp.where(rows > cols, mixed, turned))
    gram = jnp.concatenate(
        [jnp.concatenate([upper, across], axis=1), jnp.concatenate([across.T, under], axis=1)], axis=0
    )
    return gram, total[quarter : quarter + 1, HALF : 3 * HALF]


def solve_kernel(count, slot_ref, pieces_ref, ids_ref, scores_ref, domain_ref, work_ref):
    total = jnp.sum(pieces_ref[...], axis=0)
    if packs(count):
        total = [total[:, i * 128 : (i + 1) * 128] for i in range(total.shape[1] // 128)]
        raw_gram, all_domains = unpack(jnp.concatenate(total, axis=0))
    else:
        raw_gram, all_domains = total[:count], total[count : count + 1]
    rows = lax.broadcasted_iota(jnp.int32, (count, count), 0)
    cols = lax.broadcasted_iota(jnp.int32, (count, count), 1)
    on_diagonal = jnp.where(rows == cols, raw_gram, 0.0)
    gram = raw_gram * lax.rsqrt(jnp.sum(on_diagonal, axis=1, keepdims=True) + 1e-06)
    gram = gram * lax.rsqrt(jnp.sum(on_diagonal, axis=0, keepdims=True) + 1e-06)

    work_ref[...] = gram + jnp.where(rows == cols, 0.25, 0.0)
    along, down = cols[:1], rows[:, :1]

    def at(array, k):
        return jnp.sum(jnp.where(along == k, array, 0.0), axis=1, keepdims=True)

    def sweep(step, carry):
        k = 2 * step
        held = work_ref[...]
        row0, row1 = work_ref[pl.ds(k, 1), :], work_ref[pl.ds(k + 1, 1), :]
        a, b, d = at(row0, k), at(row1, k), at(row1, k + 1)
        scale = 1.0 / (a * d - b * b)
        a, b, d = a * scale, b * scale, d * scale
        column0, column1 = at(held, k), at(held, k + 1)
        new0 = jnp.where(along == k, -d, jnp.where(along == k + 1, b, d * row0 - b * row1))
        new1 = jnp.where(along == k, b, jnp.where(along == k + 1, -a, a * row1 - b * row0))
        column0 = jnp.where(down == k, -1.0, jnp.where(down == k + 1, 0.0, column0))
        column1 = jnp.where(down == k, 0.0, jnp.where(down == k + 1, -1.0, column1))
        swept = (cols == k) | (cols == k + 1) | (rows == k) | (rows == k + 1)
        work_ref[...] = jnp.where(swept, 0.0, held) - column0 * new0 - column1 * new1
        return carry

    lax.fori_loop(0, count // 2, sweep, 0)

    targets = ids_ref.shape[1]
    places = lax.broadcasted_iota(jnp.int32, (count, targets), 0)
    chosen = places == ids_ref[...]
    cross = exact_dot(gram, jnp.where(chosen, 1.0, 0.0), ((1,), (0,)))
    cross = jnp.where(chosen, 0.0, cross)
    scores = exact_dot(work_ref[...], cross, ((1,), (0,))) * -math.sqrt(K)
    kinds = lax.broadcasted_iota(jnp.int32, (DOMAINS, count), 0).astype(jnp.float32)
    indicator = jnp.where(kinds == all_domains, 1.0, 0.0)
    domain_ref[...] = exact_dot(indicator, scores, ((1,), (0,))) / math.sqrt(count / DOMAINS)
    work_ref[:, :targets] = scores
    scores_ref[...] = work_ref[pl.ds(pl.multiple_of(slot_ref[0], 8), scores_ref.shape[0]), :targets]


def solve(pieces, target_ids, slot, ex_rows, count):
    targets = target_ids.shape[0]
    return pl.pallas_call(
        functools.partial(solve_kernel, count),
        out_shape=(
            jax.ShapeDtypeStruct((ex_rows, targets), jnp.float32),
            jax.ShapeDtypeStruct((DOMAINS, targets), jnp.float32),
        ),
        in_specs=[
            pl.BlockSpec(memory_space=pltpu.SMEM),
            pl.BlockSpec(memory_space=pltpu.VMEM),
            pl.BlockSpec(memory_space=pltpu.VMEM),
        ],
        out_specs=(pl.BlockSpec(memory_space=pltpu.VMEM), pl.BlockSpec(memory_space=pltpu.VMEM)),
        scratch_shapes=[pltpu.VMEM((count, count), jnp.float32)],
        compiler_params=pltpu.CompilerParams(vmem_limit_bytes=16 << 20),
        name="solve",
    )(jnp.reshape(slot, (1,)), pieces, target_ids[None])


def local(
    activations,
    output_gradients,
    down_projection_weight,
    adapter_up,
    projection,
    domains,
    target_ids,
):
    single_float = jnp.float32
    ex_rows = activations.shape[0]
    rank = down_projection_weight.shape[1]
    ex_size = lax.axis_size("ex")
    devices = lax.axis_size("param") * ex_size
    example_count = ex_rows * ex_size

    tokens = activations.shape[1]
    channels = activations.shape[2]
    owned = channels // ex_size

    wire, partial_low = first_sums(
        activations, output_gradients, down_projection_weight, adapter_up.swapaxes(1, 2), ex_size
    )
    if wire is None:
        wire = activations.reshape(ex_rows, tokens, ex_size, owned).transpose(2, 0, 1, 3)
    moved = swap(wire, "ex").reshape(example_count, tokens, owned)

    low_parts = lax.all_gather(partial_low, "param")
    if meets(ex_size):
        queries, rest = low_columns(low_parts, 1)
        pair = jnp.concatenate([queries, flip(queries, 1)], axis=0)
        queries = [pair] + [flip(pair, bits) for bits in (2, 4, 6)]
        offset = lax.axis_index("ex")
    else:
        queries, rest = low_columns(low_parts, ex_size)
        queries, moved = lax.optimization_barrier((queries, moved))
        queries = [swap(queries, "ex")]
        offset = jnp.int32(0)

    wire = gradient_rows(output_gradients, rest, ex_size)
    queries, wire = lax.optimization_barrier((queries, wire))
    grads = swap(wire, "ex").reshape(example_count, owned * 2 * rank)
    rows = projection.reshape(owned, 4 * rank, K)
    total = early_features(moved, offset, queries, rows)

    slot = lax.axis_index("ex") * ex_rows
    mine = jnp.where(lax.axis_index("param") == 0, domains, 0).astype(single_float)
    domain_row = lax.dynamic_update_slice(jnp.zeros((example_count,), single_float), mine, (slot,))
    if packs(example_count):
        row = jnp.pad(domain_row, (HALF, 128 - HALF - example_count))[None]
        core = lax.rem(lax.axis_index("ex"), 2)
        own, other = late_features_paired(grads, rows, total, core, devices // 2)
        own = (own + flip(other, 1)).astype(jnp.bfloat16)
        piece = packed_gram(swap(own, EVERY, 2), row)
        piece = piece + flip(piece, 1)
        pieces = swap(jnp.broadcast_to(piece[None], (devices // 2, *piece.shape)), EVERY, 2)
    else:
        partial_sums = late_features(grads, rows, total)
        partial_sums = partial_sums.reshape(example_count, devices, K // devices).transpose(1, 0, 2)
        arrived = swap(partial_sums, EVERY)
        features = jnp.sum(arrived.astype(single_float), axis=0)
        gram = exact_dot(features, features, ((1,), (1,)))
        gram = jnp.concatenate([gram, jnp.broadcast_to(domain_row, (devices, example_count))], axis=0)
        share = gram.shape[0] // devices
        summed = jnp.sum(swap(gram, EVERY).reshape(devices, share, example_count), axis=0)
        pieces = swap(jnp.broadcast_to(summed[None], (devices, share, example_count)), EVERY)
        pieces = pieces.reshape(1, devices * share, example_count)
    scores, domain_scores = solve(pieces, target_ids, slot, ex_rows, example_count)
    return (scores.T, domain_scores.T)


def solution(mesh):
    in_specs = (
        P("ex", None, "param"),
        P(None, "ex", None, "param"),
        P(None, None, "param"),
        P(None, "param", None),
        P(("param", "ex"), None),
        P("ex"),
        P("param"),
    )
    out_specs = (P("param", "ex"), P("param", None))
    return jax.shard_map(local, mesh=mesh, in_specs=in_specs, out_specs=out_specs, check_vma=False)
```

```python
import functools
import math

import jax
import jax.numpy as jnp
from jax import lax
from jax.experimental import pallas as pl
from jax.experimental.pallas import tpu as pltpu
from jax.sharding import PartitionSpec as P

K = 4096
DOMAINS = 4
HALF = 32
FOLD = 4
GROUP = 8
SLOTS = 12
EVERY = ("param", "ex")


def exact_dot(left, right, dims):
    return lax.dot_general(
        left, right, (dims, ((), ())), precision=lax.Precision.HIGHEST, preferred_element_type=jnp.float32
    )


def swap(blocks, axes, groups=1):
    members = None
    if groups > 1:
        members = [list(range(i, groups * blocks.shape[0], groups)) for i in range(groups)]
    return lax.all_to_all(blocks, axes, split_axis=0, concat_axis=0, axis_index_groups=members, tiled=True)


def first_sums_kernel(blocked, *refs):
    sources, low_ref, out_ref, wire_ref = refs[:4], refs[4], refs[5], refs[6 : 6 + blocked]
    act_ref, down_ref, up_ref, sems = refs[6 + blocked :]
    held = (act_ref, out_ref, down_ref, up_ref)
    copies = [pltpu.make_async_copy(source, here, sems.at[i]) for i, (source, here) in enumerate(zip(sources, held))]
    for copy in copies:
        copy.start()
    examples, tokens, channels = act_ref.shape
    copies[0].wait()
    for wire in wire_ref:
        owned = wire.shape[3]
        for block in range(wire.shape[0]):
            wire[block] = act_ref[:, :, block * owned : (block + 1) * owned]
    for copy in copies[1:]:
        copy.wait()
    rank = down_ref.shape[1]
    inputs = act_ref[...].reshape(examples * tokens, channels)
    pairs = [(up_ref[i], out_ref[i].reshape(examples * tokens, channels)) for i in range(2)]
    pairs += [(down_ref[i], inputs) for i in range(2)]
    for i, (weight, values) in enumerate(pairs):
        low_ref[i * rank : (i + 1) * rank, :] = lax.dot_general(
            weight, values, (((1,), (1,)), ((), ())), preferred_element_type=jnp.float32
        )


def first_sums(activations, output_gradients, down, up, blocks):
    examples, tokens, channels = activations.shape
    out_shape = [
        jax.ShapeDtypeStruct((4 * down.shape[1], examples * tokens), jnp.float32),
        jax.ShapeDtypeStruct(output_gradients.shape, output_gradients.dtype),
    ]
    if channels // blocks % 128 == 0:
        out_shape.append(jax.ShapeDtypeStruct((blocks, examples, tokens, channels // blocks), activations.dtype))
    operands = (activations, output_gradients, down, up)
    kept = [pltpu.with_memory_space_constraint(operand, pltpu.HBM) for operand in operands]
    low, held, *wire = pl.pallas_call(
        functools.partial(first_sums_kernel, len(out_shape) - 2),
        out_shape=out_shape,
        in_specs=[pl.BlockSpec(memory_space=pltpu.HBM)] * 4,
        scratch_shapes=[pltpu.VMEM(operand.shape, operand.dtype) for operand in (activations, down, up)]
        + [pltpu.SemaphoreType.DMA((4,))],
        compiler_params=pltpu.CompilerParams(vmem_limit_bytes=16 << 20),
        name="first_sums",
    )(*kept)
    return (wire[0] if wire else None), low, held


def spread(columns):
    return jnp.concatenate([columns] * FOLD, axis=0).T


def meets(ex_size):
    return ex_size == 8


def low_columns_kernel(parts_ref, queries_ref, rest_ref):
    low = parts_ref[0]
    for part in range(1, parts_ref.shape[0]):
        low = low + parts_ref[part]
    low = low.astype(jnp.bfloat16)
    half = low.shape[0] // 2
    for block in range(queries_ref.shape[0]):
        queries_ref[block] = low[:half]
    rest_ref[...] = spread(low[half:].astype(jnp.float32)).astype(jnp.bfloat16)


def low_columns(parts, blocks):
    _, columns, tokens = parts.shape
    return pl.pallas_call(
        low_columns_kernel,
        out_shape=(
            jax.ShapeDtypeStruct((blocks, columns // 2, tokens), jnp.bfloat16),
            jax.ShapeDtypeStruct((tokens, FOLD * columns // 2), jnp.bfloat16),
        ),
        compiler_params=pltpu.CompilerParams(vmem_limit_bytes=16 << 20),
        name="low_columns",
    )(parts)


def fold_rows(tall_ref, first, count):
    folded = tall_ref[pl.ds(first, count // FOLD, stride=FOLD), :]
    group = lax.broadcasted_iota(jnp.int32, folded.shape, 1) // (128 // FOLD)
    for j in range(1, FOLD):
        folded = jnp.where(group == j, tall_ref[pl.ds(first + j, count // FOLD, stride=FOLD), :], folded)
    return folded


def gradient_rows_kernel(out_ref, low_ref, wire_ref, tall_ref, wide_ref):
    _, examples, tokens, channels = out_ref.shape
    blocks = wire_ref.shape[0]
    for n in range(examples):
        factors = low_ref[n * tokens : (n + 1) * tokens, :].astype(jnp.float32)
        column = lax.rem(lax.broadcasted_iota(jnp.int32, factors.shape, 1), 128 // FOLD)
        value = column >= 64 // FOLD
        factors = jnp.concatenate([jnp.where(value, 0.0, factors), jnp.where(value, factors, 0.0)], axis=0)
        both = jnp.concatenate([out_ref[0, n], out_ref[1, n]], axis=0)
        tall_ref[...] = lax.dot_general(
            both, factors.astype(jnp.bfloat16), (((0,), (0,)), ((), ())), preferred_element_type=jnp.float32
        )
        wide_ref[pl.ds(n, channels // FOLD, stride=examples), :] = fold_rows(tall_ref, 0, channels)
    tiles = channels // FOLD // blocks
    for block in range(blocks):
        for tile in range(tiles):
            start = (block * tiles + tile) * examples
            piece = wide_ref[start : start + examples, :].astype(jnp.bfloat16)
            wire_ref[block, :, tile * 128 : (tile + 1) * 128] = piece


def gradient_rows(output_gradients, low, blocks):
    _, examples, _, channels = output_gradients.shape
    lanes = channels * 128 // FOLD // blocks
    return pl.pallas_call(
        gradient_rows_kernel,
        out_shape=jax.ShapeDtypeStruct((blocks, examples, lanes), jnp.bfloat16),
        scratch_shapes=[
            pltpu.VMEM((channels, 128), jnp.float32),
            pltpu.VMEM((channels // FOLD * examples, 128), jnp.float32),
        ],
        compiler_params=pltpu.CompilerParams(vmem_limit_bytes=16 << 20),
        name="gradient_rows",
    )(output_gradients, low)


def multiply_rows(grads_ref, rows_ref, half, held_ref, sems, acc_ref, prepare, total_ref):
    slots, group, columns, _ = held_ref.shape
    size = group * columns
    count = rows_ref.shape[0] // group

    def copy(i):
        return pltpu.make_async_copy(
            rows_ref.at[pl.ds(i * group, group), pl.ds(half * columns, columns)],
            held_ref.at[i % slots],
            sems.at[i % slots],
        )

    for i in range(min(slots, count)):
        copy(i).start()
    prepare()
    for i in range(count):
        copy(i).wait()
        product = jnp.dot(
            grads_ref[:, i * size : (i + 1) * size],
            held_ref[i % slots].reshape(size, held_ref.shape[3]),
            preferred_element_type=jnp.float32,
        )
        if i:
            acc_ref[...] += product
        elif total_ref is None:
            acc_ref[...] = product
        else:
            acc_ref[...] = total_ref[...] + product
        if i + slots < count:
            copy(i + slots).start()


def early_features_kernel(parts, offset_ref, tokens_ref, *refs):
    rows_ref, total_ref, low_ref, grads_ref, tall_ref, wide_ref, held_ref, sems = refs[parts:]
    examples, length, channels = tokens_ref.shape
    sources = low_ref.shape[0]
    each = examples // sources

    def prepare():
        first = 0
        for part in refs[:parts]:
            low_ref[first : first + part.shape[0]] = part[...]
            first += part.shape[0]

        def source(index, carry):
            factors = spread(low_ref[lax.bitwise_xor(index, offset_ref[0])].astype(jnp.float32)).astype(jnp.bfloat16)
            for n in range(each):
                tall_ref[n * channels : (n + 1) * channels, :] = lax.dot_general(
                    tokens_ref[index * each + n],
                    factors[n * length : (n + 1) * length],
                    (((0,), (0,)), ((), ())),
                    preferred_element_type=jnp.float32,
                )
            for n in range(each):
                wide_ref[pl.ds(index * each + n, channels // FOLD, stride=examples), :] = fold_rows(
                    tall_ref, n * channels, channels
                )
            return carry

        lax.fori_loop(0, sources, source, 0)
        for tile in range(channels // FOLD):
            grads_ref[:, tile * 128 : (tile + 1) * 128] = wide_ref[
                tile * examples : (tile + 1) * examples, :
            ].astype(jnp.bfloat16)

    multiply_rows(grads_ref, rows_ref, 0, held_ref, sems, total_ref, prepare, None)


def held_rows(rows):
    return [
        pltpu.VMEM((SLOTS, GROUP, rows.shape[1] // 2, rows.shape[2]), rows.dtype),
        pltpu.SemaphoreType.DMA((SLOTS,)),
    ]


def early_features(tokens, offset, low, rows):
    examples, _, channels = tokens.shape
    sources = sum(part.shape[0] for part in low)
    in_vmem = pl.BlockSpec(memory_space=pltpu.VMEM)
    return pl.pallas_call(
        functools.partial(early_features_kernel, len(low)),
        out_shape=jax.ShapeDtypeStruct((examples, rows.shape[2]), jnp.float32),
        in_specs=[pl.BlockSpec(memory_space=pltpu.SMEM), in_vmem]
        + [in_vmem] * len(low)
        + [pl.BlockSpec(memory_space=pl.ANY)],
        out_specs=in_vmem,
        scratch_shapes=[
            pltpu.VMEM((sources, *low[0].shape[1:]), jnp.bfloat16),
            pltpu.VMEM((examples, channels * 128 // FOLD), jnp.bfloat16),
            pltpu.VMEM((examples // sources * channels, 128), jnp.float32),
            pltpu.VMEM((channels // FOLD * examples, 128), jnp.float32),
        ]
        + held_rows(rows),
        compiler_params=pltpu.CompilerParams(vmem_limit_bytes=40 << 20),
        name="early_features",
    )(jnp.reshape(offset, (1,)), tokens, *low, rows)


def late_features_kernel(grads_ref, rows_ref, total_ref, out_ref, acc_ref, held_ref, sems):
    multiply_rows(grads_ref, rows_ref, 1, held_ref, sems, acc_ref, lambda: None, total_ref)
    out_ref[...] = acc_ref[...].astype(out_ref.dtype)


def late_features_paired_kernel(core_ref, grads_ref, rows_ref, total_ref, own_ref, other_ref, acc_ref, held_ref, sems):
    multiply_rows(grads_ref, rows_ref, 1, held_ref, sems, acc_ref, lambda: None, total_ref)
    pairs, _, lanes = own_ref.shape
    first = core_ref[0] == 0
    for pair in range(pairs):
        even = acc_ref[:, 2 * pair * lanes : (2 * pair + 1) * lanes]
        odd = acc_ref[:, (2 * pair + 1) * lanes : (2 * pair + 2) * lanes]
        own_ref[pair] = jnp.where(first, even, odd)
        other_ref[pair] = jnp.where(first, odd, even)


def late_features_paired(grads, rows, total, core, pairs):
    examples, columns = total.shape
    in_vmem = pl.BlockSpec(memory_space=pltpu.VMEM)
    shape = jax.ShapeDtypeStruct((pairs, examples, columns // pairs // 2), jnp.float32)
    return pl.pallas_call(
        late_features_paired_kernel,
        out_shape=(shape, shape),
        in_specs=[pl.BlockSpec(memory_space=pltpu.SMEM), in_vmem, pl.BlockSpec(memory_space=pl.ANY), in_vmem],
        out_specs=(in_vmem, in_vmem),
        scratch_shapes=[pltpu.VMEM((examples, columns), jnp.float32)] + held_rows(rows),
        compiler_params=pltpu.CompilerParams(vmem_limit_bytes=40 << 20),
        name="late_features",
    )(jnp.reshape(core, (1,)), grads, rows, total)


def late_features(grads, rows, total):
    examples, columns = total.shape
    shape = (examples, columns)
    in_vmem = pl.BlockSpec(memory_space=pltpu.VMEM)
    return pl.pallas_call(
        late_features_kernel,
        out_shape=jax.ShapeDtypeStruct(shape, jnp.bfloat16),
        in_specs=[in_vmem, pl.BlockSpec(memory_space=pl.ANY), in_vmem],
        out_specs=in_vmem,
        scratch_shapes=[pltpu.VMEM((examples, columns), jnp.float32)] + held_rows(rows),
        compiler_params=pltpu.CompilerParams(vmem_limit_bytes=40 << 20),
        name="late_features",
    )(grads, rows, total)


def flip(array, bits):
    return lax.ppermute(array, "ex", [(i, i ^ bits) for i in range(lax.axis_size("ex"))])


def packs(example_count):
    return example_count == 2 * HALF


def packed_gram_kernel(blocks_ref, row_ref, out_ref):
    features = jnp.sum(blocks_ref[...].astype(jnp.float32), axis=0)
    gram = exact_dot(features, features, ((1,), (1,)))
    upper, across, under = gram[:HALF, :HALF], gram[:HALF, HALF:], gram[HALF:, HALF:]
    rows = lax.broadcasted_iota(jnp.int32, (HALF, HALF), 0)
    cols = lax.broadcasted_iota(jnp.int32, (HALF, HALF), 1)
    mixed = jnp.where(rows <= cols, upper, under)
    quarter = HALF // 2
    body = jnp.concatenate([across[:quarter], across[quarter:], mixed[:quarter], mixed[quarter:]], axis=1)
    diagonal = jnp.sum(jnp.where(rows == cols, under, 0.0), axis=0, keepdims=True)
    last = row_ref[...] + jnp.concatenate([diagonal, jnp.zeros((1, 128 - HALF), jnp.float32)], axis=1)
    for i in range(quarter):
        out_ref[:, i * 128 : (i + 1) * 128] = body[i : i + 1]
    out_ref[:, quarter * 128 :] = last


def packed_gram(blocks, row):
    return pl.pallas_call(
        packed_gram_kernel,
        out_shape=jax.ShapeDtypeStruct((1, (HALF // 2 + 1) * 128), jnp.float32),
        compiler_params=pltpu.CompilerParams(vmem_limit_bytes=16 << 20),
        name="packed_gram",
    )(blocks, row)


def unpack(total):
    quarter = HALF // 2
    rows = lax.broadcasted_iota(jnp.int32, (HALF, HALF), 0)
    cols = lax.broadcasted_iota(jnp.int32, (HALF, HALF), 1)
    body = total[:quarter]
    across = jnp.concatenate([body[:, :HALF], body[:, HALF : 2 * HALF]], axis=0)
    mixed = jnp.concatenate([body[:, 2 * HALF : 3 * HALF], body[:, 3 * HALF :]], axis=0)
    turned = mixed.T
    upper = jnp.where(rows <= cols, mixed, turned)
    diagonal = jnp.broadcast_to(total[quarter : quarter + 1, :HALF], (HALF, HALF))
    under = jnp.where(rows == cols, diagonal, jnp.where(rows > cols, mixed, turned))
    gram = jnp.concatenate(
        [jnp.concatenate([upper, across], axis=1), jnp.concatenate([across.T, under], axis=1)], axis=0
    )
    return gram, total[quarter : quarter + 1, HALF : 3 * HALF]


def solve_kernel(count, slot_ref, pieces_ref, ids_ref, scores_ref, domain_ref, work_ref):
    total = jnp.sum(pieces_ref[...], axis=0)
    if packs(count):
        total = [total[:, i * 128 : (i + 1) * 128] for i in range(total.shape[1] // 128)]
        raw_gram, all_domains = unpack(jnp.concatenate(total, axis=0))
    else:
        raw_gram, all_domains = total[:count], total[count : count + 1]
    rows = lax.broadcasted_iota(jnp.int32, (count, count), 0)
    cols = lax.broadcasted_iota(jnp.int32, (count, count), 1)
    on_diagonal = jnp.where(rows == cols, raw_gram, 0.0)
    gram = raw_gram * lax.rsqrt(jnp.sum(on_diagonal, axis=1, keepdims=True) + 1e-06)
    gram = gram * lax.rsqrt(jnp.sum(on_diagonal, axis=0, keepdims=True) + 1e-06)

    work_ref[...] = gram + jnp.where(rows == cols, 0.25, 0.0)
    along, down = cols[:1], rows[:, :1]

    def at(array, k):
        return jnp.sum(jnp.where(along == k, array, 0.0), axis=1, keepdims=True)

    def sweep(step, carry):
        k = 2 * step
        held = work_ref[...]
        row0, row1 = work_ref[pl.ds(k, 1), :], work_ref[pl.ds(k + 1, 1), :]
        a, b, d = at(row0, k), at(row1, k), at(row1, k + 1)
        scale = 1.0 / (a * d - b * b)
        a, b, d = a * scale, b * scale, d * scale
        column0, column1 = at(held, k), at(held, k + 1)
        new0 = jnp.where(along == k, -d, jnp.where(along == k + 1, b, d * row0 - b * row1))
        new1 = jnp.where(along == k, b, jnp.where(along == k + 1, -a, a * row1 - b * row0))
        column0 = jnp.where(down == k, -1.0, jnp.where(down == k + 1, 0.0, column0))
        column1 = jnp.where(down == k, 0.0, jnp.where(down == k + 1, -1.0, column1))
        swept = (cols == k) | (cols == k + 1) | (rows == k) | (rows == k + 1)
        work_ref[...] = jnp.where(swept, 0.0, held) - column0 * new0 - column1 * new1
        return carry

    lax.fori_loop(0, count // 2, sweep, 0)

    targets = ids_ref.shape[1]
    places = lax.broadcasted_iota(jnp.int32, (count, targets), 0)
    chosen = places == ids_ref[...]
    cross = exact_dot(gram, jnp.where(chosen, 1.0, 0.0), ((1,), (0,)))
    cross = jnp.where(chosen, 0.0, cross)
    scores = exact_dot(work_ref[...], cross, ((1,), (0,))) * -math.sqrt(K)
    kinds = lax.broadcasted_iota(jnp.int32, (DOMAINS, count), 0).astype(jnp.float32)
    indicator = jnp.where(kinds == all_domains, 1.0, 0.0)
    domain_ref[...] = exact_dot(indicator, scores, ((1,), (0,))) / math.sqrt(count / DOMAINS)
    work_ref[:, :targets] = scores
    scores_ref[...] = work_ref[pl.ds(pl.multiple_of(slot_ref[0], 8), scores_ref.shape[0]), :targets]


def solve(pieces, target_ids, slot, ex_rows, count):
    targets = target_ids.shape[0]
    return pl.pallas_call(
        functools.partial(solve_kernel, count),
        out_shape=(
            jax.ShapeDtypeStruct((ex_rows, targets), jnp.float32),
            jax.ShapeDtypeStruct((DOMAINS, targets), jnp.float32),
        ),
        in_specs=[
            pl.BlockSpec(memory_space=pltpu.SMEM),
            pl.BlockSpec(memory_space=pltpu.VMEM),
            pl.BlockSpec(memory_space=pltpu.VMEM),
        ],
        out_specs=(pl.BlockSpec(memory_space=pltpu.VMEM), pl.BlockSpec(memory_space=pltpu.VMEM)),
        scratch_shapes=[pltpu.VMEM((count, count), jnp.float32)],
        compiler_params=pltpu.CompilerParams(vmem_limit_bytes=16 << 20),
        name="solve",
    )(jnp.reshape(slot, (1,)), pieces, target_ids[None])


def local(
    activations,
    output_gradients,
    down_projection_weight,
    adapter_up,
    projection,
    domains,
    target_ids,
):
    single_float = jnp.float32
    ex_rows = activations.shape[0]
    rank = down_projection_weight.shape[1]
    ex_size = lax.axis_size("ex")
    devices = lax.axis_size("param") * ex_size
    example_count = ex_rows * ex_size

    tokens = activations.shape[1]
    channels = activations.shape[2]
    owned = channels // ex_size

    wire, partial_low, held = first_sums(
        activations, output_gradients, down_projection_weight, adapter_up.swapaxes(1, 2), ex_size
    )
    if wire is None:
        wire = activations.reshape(ex_rows, tokens, ex_size, owned).transpose(2, 0, 1, 3)
    moved = swap(wire, "ex").reshape(example_count, tokens, owned)

    low_parts = lax.all_gather(partial_low, "param")
    if meets(ex_size):
        queries, rest = low_columns(low_parts, 1)
        pair = jnp.concatenate([queries, flip(queries, 1)], axis=0)
        queries = [pair] + [flip(pair, bits) for bits in (2, 4, 6)]
        offset = lax.axis_index("ex")
    else:
        queries, rest = low_columns(low_parts, ex_size)
        queries, moved = lax.optimization_barrier((queries, moved))
        queries = [swap(queries, "ex")]
        offset = jnp.int32(0)

    wire = gradient_rows(held, rest, ex_size)
    queries, wire = lax.optimization_barrier((queries, wire))
    grads = swap(wire, "ex").reshape(example_count, owned * 2 * rank)
    rows = projection.reshape(owned, 4 * rank, K)
    total = early_features(moved, offset, queries, rows)

    slot = lax.axis_index("ex") * ex_rows
    mine = jnp.where(lax.axis_index("param") == 0, domains, 0).astype(single_float)
    domain_row = lax.dynamic_update_slice(jnp.zeros((example_count,), single_float), mine, (slot,))
    if packs(example_count):
        row = jnp.pad(domain_row, (HALF, 128 - HALF - example_count))[None]
        core = lax.rem(lax.axis_index("ex"), 2)
        own, other = late_features_paired(grads, rows, total, core, devices // 2)
        own = (own + flip(other, 1)).astype(jnp.bfloat16)
        piece = packed_gram(swap(own, EVERY, 2), row)
        piece = piece + flip(piece, 1)
        pieces = swap(jnp.broadcast_to(piece[None], (devices // 2, *piece.shape)), EVERY, 2)
    else:
        partial_sums = late_features(grads, rows, total)
        partial_sums = partial_sums.reshape(example_count, devices, K // devices).transpose(1, 0, 2)
        arrived = swap(partial_sums, EVERY)
        features = jnp.sum(arrived.astype(single_float), axis=0)
        gram = exact_dot(features, features, ((1,), (1,)))
        gram = jnp.concatenate([gram, jnp.broadcast_to(domain_row, (devices, example_count))], axis=0)
        share = gram.shape[0] // devices
        summed = jnp.sum(swap(gram, EVERY).reshape(devices, share, example_count), axis=0)
        pieces = swap(jnp.broadcast_to(summed[None], (devices, share, example_count)), EVERY)
        pieces = pieces.reshape(1, devices * share, example_count)
    scores, domain_scores = solve(pieces, target_ids, slot, ex_rows, example_count)
    return (scores.T, domain_scores.T)


def solution(mesh):
    in_specs = (
        P("ex", None, "param"),
        P(None, "ex", None, "param"),
        P(None, None, "param"),
        P(None, "param", None),
        P(("param", "ex"), None),
        P("ex"),
        P("param"),
    )
    out_specs = (P("param", "ex"), P("param", None))
    return jax.shard_map(local, mesh=mesh, in_specs=in_specs, out_specs=out_specs, check_vma=False)
```

```python
import functools
import math

import jax
import jax.numpy as jnp
from jax import lax
from jax.experimental import pallas as pl
from jax.experimental.pallas import tpu as pltpu
from jax.sharding import PartitionSpec as P

K = 4096
DOMAINS = 4
HALF = 32
FOLD = 4
GROUP = 8
SLOTS = 12
EVERY = ("param", "ex")


def exact_dot(left, right, dims):
    return lax.dot_general(
        left, right, (dims, ((), ())), precision=lax.Precision.HIGHEST, preferred_element_type=jnp.float32
    )


def swap(blocks, axes, groups=1):
    members = None
    if groups > 1:
        members = [list(range(i, groups * blocks.shape[0], groups)) for i in range(groups)]
    return lax.all_to_all(blocks, axes, split_axis=0, concat_axis=0, axis_index_groups=members, tiled=True)


def first_sums_kernel(blocked, *refs):
    sources, low_ref, out_ref, wire_ref = refs[:4], refs[4], refs[5], refs[6 : 6 + blocked]
    act_ref, down_ref, up_ref, sems = refs[6 + blocked :]
    held = (act_ref, out_ref, down_ref, up_ref)
    copies = [pltpu.make_async_copy(source, here, sems.at[i]) for i, (source, here) in enumerate(zip(sources, held))]
    for copy in copies:
        copy.start()
    examples, tokens, channels = act_ref.shape
    copies[0].wait()
    for wire in wire_ref:
        owned = wire.shape[3]
        for block in range(wire.shape[0]):
            wire[block] = act_ref[:, :, block * owned : (block + 1) * owned]
    for copy in copies[1:]:
        copy.wait()
    rank = down_ref.shape[1]
    inputs = act_ref[...].reshape(examples * tokens, channels)
    pairs = [(up_ref[i], out_ref[i].reshape(examples * tokens, channels)) for i in range(2)]
    pairs += [(down_ref[i], inputs) for i in range(2)]
    for i, (weight, values) in enumerate(pairs):
        low_ref[i * rank : (i + 1) * rank, :] = lax.dot_general(
            weight, values, (((1,), (1,)), ((), ())), preferred_element_type=jnp.float32
        )


def first_sums(activations, output_gradients, down, up, blocks):
    examples, tokens, channels = activations.shape
    out_shape = [
        jax.ShapeDtypeStruct((4 * down.shape[1], examples * tokens), jnp.float32),
        jax.ShapeDtypeStruct(output_gradients.shape, output_gradients.dtype),
    ]
    if channels // blocks % 128 == 0:
        out_shape.append(jax.ShapeDtypeStruct((blocks, examples, tokens, channels // blocks), activations.dtype))
    operands = (activations, output_gradients, down, up)
    kept = [pltpu.with_memory_space_constraint(operand, pltpu.HBM) for operand in operands]
    low, held, *wire = pl.pallas_call(
        functools.partial(first_sums_kernel, len(out_shape) - 2),
        out_shape=out_shape,
        in_specs=[pl.BlockSpec(memory_space=pltpu.HBM)] * 4,
        scratch_shapes=[pltpu.VMEM(operand.shape, operand.dtype) for operand in (activations, down, up)]
        + [pltpu.SemaphoreType.DMA((4,))],
        compiler_params=pltpu.CompilerParams(vmem_limit_bytes=16 << 20),
        name="first_sums",
    )(*kept)
    return (wire[0] if wire else None), low, held


def spread(columns):
    return jnp.concatenate([columns] * FOLD, axis=0).T


def meets(ex_size):
    return ex_size == 8


def low_columns_kernel(parts_ref, queries_ref, rest_ref):
    low = parts_ref[0]
    for part in range(1, parts_ref.shape[0]):
        low = low + parts_ref[part]
    low = low.astype(jnp.bfloat16)
    half = low.shape[0] // 2
    for block in range(queries_ref.shape[0]):
        queries_ref[block] = low[:half]
    rest_ref[...] = spread(low[half:].astype(jnp.float32)).astype(jnp.bfloat16)


def low_columns(parts, blocks):
    _, columns, tokens = parts.shape
    return pl.pallas_call(
        low_columns_kernel,
        out_shape=(
            jax.ShapeDtypeStruct((blocks, columns // 2, tokens), jnp.bfloat16),
            jax.ShapeDtypeStruct((tokens, FOLD * columns // 2), jnp.bfloat16),
        ),
        compiler_params=pltpu.CompilerParams(vmem_limit_bytes=16 << 20),
        name="low_columns",
    )(parts)


def fold_rows(tall_ref, first, count):
    folded = tall_ref[pl.ds(first, count // FOLD, stride=FOLD), :]
    group = lax.broadcasted_iota(jnp.int32, folded.shape, 1) // (128 // FOLD)
    for j in range(1, FOLD):
        folded = jnp.where(group == j, tall_ref[pl.ds(first + j, count // FOLD, stride=FOLD), :], folded)
    return folded


def gradient_rows_kernel(out_ref, low_ref, wire_ref, tall_ref, wide_ref):
    _, examples, tokens, channels = out_ref.shape
    blocks = wire_ref.shape[0]
    for n in range(examples):
        factors = low_ref[n * tokens : (n + 1) * tokens, :].astype(jnp.float32)
        column = lax.rem(lax.broadcasted_iota(jnp.int32, factors.shape, 1), 128 // FOLD)
        value = column >= 64 // FOLD
        factors = jnp.concatenate([jnp.where(value, 0.0, factors), jnp.where(value, factors, 0.0)], axis=0)
        both = jnp.concatenate([out_ref[0, n], out_ref[1, n]], axis=0)
        tall_ref[...] = lax.dot_general(
            both, factors.astype(jnp.bfloat16), (((0,), (0,)), ((), ())), preferred_element_type=jnp.float32
        )
        wide_ref[pl.ds(n, channels // FOLD, stride=examples), :] = fold_rows(tall_ref, 0, channels)
    tiles = channels // FOLD // blocks
    for block in range(blocks):
        for tile in range(tiles):
            start = (block * tiles + tile) * examples
            piece = wide_ref[start : start + examples, :].astype(jnp.bfloat16)
            wire_ref[block, :, tile * 128 : (tile + 1) * 128] = piece


def gradient_rows(output_gradients, low, blocks):
    _, examples, _, channels = output_gradients.shape
    lanes = channels * 128 // FOLD // blocks
    return pl.pallas_call(
        gradient_rows_kernel,
        out_shape=jax.ShapeDtypeStruct((blocks, examples, lanes), jnp.bfloat16),
        scratch_shapes=[
            pltpu.VMEM((channels, 128), jnp.float32),
            pltpu.VMEM((channels // FOLD * examples, 128), jnp.float32),
        ],
        compiler_params=pltpu.CompilerParams(vmem_limit_bytes=16 << 20),
        name="gradient_rows",
    )(output_gradients, low)


def multiply_rows(grads_ref, rows_ref, half, held_ref, sems, acc_ref, prepare, total_ref):
    slots, group, columns, _ = held_ref.shape
    size = group * columns
    count = rows_ref.shape[0] // group

    def copy(i):
        return pltpu.make_async_copy(
            rows_ref.at[pl.ds(i * group, group), pl.ds(half * columns, columns)],
            held_ref.at[i % slots],
            sems.at[i % slots],
        )

    for i in range(min(slots, count)):
        copy(i).start()
    prepare()
    for i in range(count):
        copy(i).wait()
        product = jnp.dot(
            grads_ref[:, i * size : (i + 1) * size],
            held_ref[i % slots].reshape(size, held_ref.shape[3]),
            preferred_element_type=jnp.float32,
        )
        if i:
            acc_ref[...] += product
        elif total_ref is None:
            acc_ref[...] = product
        else:
            acc_ref[...] = total_ref[...] + product
        if i + slots < count:
            copy(i + slots).start()


def early_features_kernel(parts, offset_ref, tokens_ref, *refs):
    rows_ref, total_ref, low_ref, grads_ref, tall_ref, wide_ref, held_ref, sems = refs[parts:]
    examples, length, channels = tokens_ref.shape
    sources = low_ref.shape[0]
    each = examples // sources

    def prepare():
        first = 0
        for part in refs[:parts]:
            low_ref[first : first + part.shape[0]] = part[...]
            first += part.shape[0]

        def source(index, carry):
            factors = spread(low_ref[lax.bitwise_xor(index, offset_ref[0])].astype(jnp.float32)).astype(jnp.bfloat16)
            for n in range(each):
                tall_ref[n * channels : (n + 1) * channels, :] = lax.dot_general(
                    tokens_ref[index * each + n],
                    factors[n * length : (n + 1) * length],
                    (((0,), (0,)), ((), ())),
                    preferred_element_type=jnp.float32,
                )
            for n in range(each):
                wide_ref[pl.ds(index * each + n, channels // FOLD, stride=examples), :] = fold_rows(
                    tall_ref, n * channels, channels
                )
            return carry

        lax.fori_loop(0, sources, source, 0)
        for tile in range(channels // FOLD):
            grads_ref[:, tile * 128 : (tile + 1) * 128] = wide_ref[
                tile * examples : (tile + 1) * examples, :
            ].astype(jnp.bfloat16)

    multiply_rows(grads_ref, rows_ref, 0, held_ref, sems, total_ref, prepare, None)


def held_rows(rows):
    return [
        pltpu.VMEM((SLOTS, GROUP, rows.shape[1] // 2, rows.shape[2]), rows.dtype),
        pltpu.SemaphoreType.DMA((SLOTS,)),
    ]


def early_features(tokens, offset, low, rows):
    examples, _, channels = tokens.shape
    sources = sum(part.shape[0] for part in low)
    in_vmem = pl.BlockSpec(memory_space=pltpu.VMEM)
    return pl.pallas_call(
        functools.partial(early_features_kernel, len(low)),
        out_shape=jax.ShapeDtypeStruct((examples, rows.shape[2]), jnp.float32),
        in_specs=[pl.BlockSpec(memory_space=pltpu.SMEM), in_vmem]
        + [in_vmem] * len(low)
        + [pl.BlockSpec(memory_space=pl.ANY)],
        out_specs=in_vmem,
        scratch_shapes=[
            pltpu.VMEM((sources, *low[0].shape[1:]), jnp.bfloat16),
            pltpu.VMEM((examples, channels * 128 // FOLD), jnp.bfloat16),
            pltpu.VMEM((examples // sources * channels, 128), jnp.float32),
            pltpu.VMEM((channels // FOLD * examples, 128), jnp.float32),
        ]
        + held_rows(rows),
        compiler_params=pltpu.CompilerParams(vmem_limit_bytes=40 << 20),
        name="early_features",
    )(jnp.reshape(offset, (1,)), tokens, *low, rows)


def late_features_kernel(grads_ref, rows_ref, total_ref, out_ref, acc_ref, held_ref, sems):
    multiply_rows(grads_ref, rows_ref, 1, held_ref, sems, acc_ref, lambda: None, total_ref)
    out_ref[...] = acc_ref[...].astype(out_ref.dtype)


def late_features_paired_kernel(core_ref, grads_ref, rows_ref, total_ref, own_ref, other_ref, acc_ref, held_ref, sems):
    multiply_rows(grads_ref, rows_ref, 1, held_ref, sems, acc_ref, lambda: None, total_ref)
    pairs, _, lanes = own_ref.shape
    first = core_ref[0] == 0
    for pair in range(pairs):
        even = acc_ref[:, 2 * pair * lanes : (2 * pair + 1) * lanes]
        odd = acc_ref[:, (2 * pair + 1) * lanes : (2 * pair + 2) * lanes]
        own_ref[pair] = jnp.where(first, even, odd)
        other_ref[pair] = jnp.where(first, odd, even).astype(other_ref.dtype)


def late_features_paired(grads, rows, total, core, pairs):
    examples, columns = total.shape
    in_vmem = pl.BlockSpec(memory_space=pltpu.VMEM)
    shape = (pairs, examples, columns // pairs // 2)
    return pl.pallas_call(
        late_features_paired_kernel,
        out_shape=(jax.ShapeDtypeStruct(shape, jnp.float32), jax.ShapeDtypeStruct(shape, jnp.bfloat16)),
        in_specs=[pl.BlockSpec(memory_space=pltpu.SMEM), in_vmem, pl.BlockSpec(memory_space=pl.ANY), in_vmem],
        out_specs=(in_vmem, in_vmem),
        scratch_shapes=[pltpu.VMEM((examples, columns), jnp.float32)] + held_rows(rows),
        compiler_params=pltpu.CompilerParams(vmem_limit_bytes=40 << 20),
        name="late_features",
    )(jnp.reshape(core, (1,)), grads, rows, total)


def late_features(grads, rows, total):
    examples, columns = total.shape
    shape = (examples, columns)
    in_vmem = pl.BlockSpec(memory_space=pltpu.VMEM)
    return pl.pallas_call(
        late_features_kernel,
        out_shape=jax.ShapeDtypeStruct(shape, jnp.bfloat16),
        in_specs=[in_vmem, pl.BlockSpec(memory_space=pl.ANY), in_vmem],
        out_specs=in_vmem,
        scratch_shapes=[pltpu.VMEM((examples, columns), jnp.float32)] + held_rows(rows),
        compiler_params=pltpu.CompilerParams(vmem_limit_bytes=40 << 20),
        name="late_features",
    )(grads, rows, total)


def flip(array, bits):
    return lax.ppermute(array, "ex", [(i, i ^ bits) for i in range(lax.axis_size("ex"))])


def packs(example_count):
    return example_count == 2 * HALF


def packed_gram_kernel(blocks_ref, row_ref, out_ref):
    features = jnp.sum(blocks_ref[...].astype(jnp.float32), axis=0)
    gram = exact_dot(features, features, ((1,), (1,)))
    upper, across, under = gram[:HALF, :HALF], gram[:HALF, HALF:], gram[HALF:, HALF:]
    rows = lax.broadcasted_iota(jnp.int32, (HALF, HALF), 0)
    cols = lax.broadcasted_iota(jnp.int32, (HALF, HALF), 1)
    mixed = jnp.where(rows <= cols, upper, under)
    quarter = HALF // 2
    body = jnp.concatenate([across[:quarter], across[quarter:], mixed[:quarter], mixed[quarter:]], axis=1)
    diagonal = jnp.sum(jnp.where(rows == cols, under, 0.0), axis=0, keepdims=True)
    last = row_ref[...] + jnp.concatenate([diagonal, jnp.zeros((1, 128 - HALF), jnp.float32)], axis=1)
    for i in range(quarter):
        out_ref[:, i * 128 : (i + 1) * 128] = body[i : i + 1]
    out_ref[:, quarter * 128 :] = last


def packed_gram(blocks, row):
    return pl.pallas_call(
        packed_gram_kernel,
        out_shape=jax.ShapeDtypeStruct((1, (HALF // 2 + 1) * 128), jnp.float32),
        compiler_params=pltpu.CompilerParams(vmem_limit_bytes=16 << 20),
        name="packed_gram",
    )(blocks, row)


def unpack(total):
    quarter = HALF // 2
    rows = lax.broadcasted_iota(jnp.int32, (HALF, HALF), 0)
    cols = lax.broadcasted_iota(jnp.int32, (HALF, HALF), 1)
    body = total[:quarter]
    across = jnp.concatenate([body[:, :HALF], body[:, HALF : 2 * HALF]], axis=0)
    mixed = jnp.concatenate([body[:, 2 * HALF : 3 * HALF], body[:, 3 * HALF :]], axis=0)
    turned = mixed.T
    upper = jnp.where(rows <= cols, mixed, turned)
    diagonal = jnp.broadcast_to(total[quarter : quarter + 1, :HALF], (HALF, HALF))
    under = jnp.where(rows == cols, diagonal, jnp.where(rows > cols, mixed, turned))
    gram = jnp.concatenate(
        [jnp.concatenate([upper, across], axis=1), jnp.concatenate([across.T, under], axis=1)], axis=0
    )
    return gram, total[quarter : quarter + 1, HALF : 3 * HALF]


def solve_kernel(count, slot_ref, pieces_ref, ids_ref, scores_ref, domain_ref, work_ref):
    total = jnp.sum(pieces_ref[...], axis=0)
    if packs(count):
        total = [total[:, i * 128 : (i + 1) * 128] for i in range(total.shape[1] // 128)]
        raw_gram, all_domains = unpack(jnp.concatenate(total, axis=0))
    else:
        raw_gram, all_domains = total[:count], total[count : count + 1]
    rows = lax.broadcasted_iota(jnp.int32, (count, count), 0)
    cols = lax.broadcasted_iota(jnp.int32, (count, count), 1)
    on_diagonal = jnp.where(rows == cols, raw_gram, 0.0)
    gram = raw_gram * lax.rsqrt(jnp.sum(on_diagonal, axis=1, keepdims=True) + 1e-06)
    gram = gram * lax.rsqrt(jnp.sum(on_diagonal, axis=0, keepdims=True) + 1e-06)

    work_ref[...] = gram + jnp.where(rows == cols, 0.25, 0.0)
    along, down = cols[:1], rows[:, :1]

    def at(array, k):
        return jnp.sum(jnp.where(along == k, array, 0.0), axis=1, keepdims=True)

    def sweep(step, carry):
        k = 2 * step
        held = work_ref[...]
        row0, row1 = work_ref[pl.ds(k, 1), :], work_ref[pl.ds(k + 1, 1), :]
        a, b, d = at(row0, k), at(row1, k), at(row1, k + 1)
        scale = 1.0 / (a * d - b * b)
        a, b, d = a * scale, b * scale, d * scale
        column0, column1 = at(held, k), at(held, k + 1)
        new0 = jnp.where(along == k, -d, jnp.where(along == k + 1, b, d * row0 - b * row1))
        new1 = jnp.where(along == k, b, jnp.where(along == k + 1, -a, a * row1 - b * row0))
        column0 = jnp.where(down == k, -1.0, jnp.where(down == k + 1, 0.0, column0))
        column1 = jnp.where(down == k, 0.0, jnp.where(down == k + 1, -1.0, column1))
        swept = (cols == k) | (cols == k + 1) | (rows == k) | (rows == k + 1)
        work_ref[...] = jnp.where(swept, 0.0, held) - column0 * new0 - column1 * new1
        return carry

    lax.fori_loop(0, count // 2, sweep, 0)

    targets = ids_ref.shape[1]
    places = lax.broadcasted_iota(jnp.int32, (count, targets), 0)
    chosen = places == ids_ref[...]
    cross = exact_dot(gram, jnp.where(chosen, 1.0, 0.0), ((1,), (0,)))
    cross = jnp.where(chosen, 0.0, cross)
    scores = exact_dot(work_ref[...], cross, ((1,), (0,))) * -math.sqrt(K)
    kinds = lax.broadcasted_iota(jnp.int32, (DOMAINS, count), 0).astype(jnp.float32)
    indicator = jnp.where(kinds == all_domains, 1.0, 0.0)
    domain_ref[...] = exact_dot(indicator, scores, ((1,), (0,))) / math.sqrt(count / DOMAINS)
    work_ref[:, :targets] = scores
    scores_ref[...] = work_ref[pl.ds(pl.multiple_of(slot_ref[0], 8), scores_ref.shape[0]), :targets]


def solve(pieces, target_ids, slot, ex_rows, count):
    targets = target_ids.shape[0]
    return pl.pallas_call(
        functools.partial(solve_kernel, count),
        out_shape=(
            jax.ShapeDtypeStruct((ex_rows, targets), jnp.float32),
            jax.ShapeDtypeStruct((DOMAINS, targets), jnp.float32),
        ),
        in_specs=[
            pl.BlockSpec(memory_space=pltpu.SMEM),
            pl.BlockSpec(memory_space=pltpu.VMEM),
            pl.BlockSpec(memory_space=pltpu.VMEM),
        ],
        out_specs=(pl.BlockSpec(memory_space=pltpu.VMEM), pl.BlockSpec(memory_space=pltpu.VMEM)),
        scratch_shapes=[pltpu.VMEM((count, count), jnp.float32)],
        compiler_params=pltpu.CompilerParams(vmem_limit_bytes=16 << 20),
        name="solve",
    )(jnp.reshape(slot, (1,)), pieces, target_ids[None])


def local(
    activations,
    output_gradients,
    down_projection_weight,
    adapter_up,
    projection,
    domains,
    target_ids,
):
    single_float = jnp.float32
    ex_rows = activations.shape[0]
    rank = down_projection_weight.shape[1]
    ex_size = lax.axis_size("ex")
    devices = lax.axis_size("param") * ex_size
    example_count = ex_rows * ex_size

    tokens = activations.shape[1]
    channels = activations.shape[2]
    owned = channels // ex_size

    wire, partial_low, held = first_sums(
        activations, output_gradients, down_projection_weight, adapter_up.swapaxes(1, 2), ex_size
    )
    if wire is None:
        wire = activations.reshape(ex_rows, tokens, ex_size, owned).transpose(2, 0, 1, 3)
    moved = swap(wire, "ex").reshape(example_count, tokens, owned)

    low_parts = lax.all_gather(partial_low, "param")
    if meets(ex_size):
        queries, rest = low_columns(low_parts, 1)
        pair = jnp.concatenate([queries, flip(queries, 1)], axis=0)
        queries = [pair] + [flip(pair, bits) for bits in (2, 4, 6)]
        offset = lax.axis_index("ex")
    else:
        queries, rest = low_columns(low_parts, ex_size)
        queries, moved = lax.optimization_barrier((queries, moved))
        queries = [swap(queries, "ex")]
        offset = jnp.int32(0)

    wire = gradient_rows(held, rest, ex_size)
    queries, wire = lax.optimization_barrier((queries, wire))
    grads = swap(wire, "ex").reshape(example_count, owned * 2 * rank)
    rows = projection.reshape(owned, 4 * rank, K)
    total = early_features(moved, offset, queries, rows)

    slot = lax.axis_index("ex") * ex_rows
    mine = jnp.where(lax.axis_index("param") == 0, domains, 0).astype(single_float)
    domain_row = lax.dynamic_update_slice(jnp.zeros((example_count,), single_float), mine, (slot,))
    if packs(example_count):
        row = jnp.pad(domain_row, (HALF, 128 - HALF - example_count))[None]
        core = lax.rem(lax.axis_index("ex"), 2)
        own, other = late_features_paired(grads, rows, total, core, devices // 2)
        own = (own + flip(other, 1).astype(single_float)).astype(jnp.bfloat16)
        piece = packed_gram(swap(own, EVERY, 2), row)
        piece = piece + flip(piece, 1)
        pieces = swap(jnp.broadcast_to(piece[None], (devices // 2, *piece.shape)), EVERY, 2)
    else:
        partial_sums = late_features(grads, rows, total)
        partial_sums = partial_sums.reshape(example_count, devices, K // devices).transpose(1, 0, 2)
        arrived = swap(partial_sums, EVERY)
        features = jnp.sum(arrived.astype(single_float), axis=0)
        gram = exact_dot(features, features, ((1,), (1,)))
        gram = jnp.concatenate([gram, jnp.broadcast_to(domain_row, (devices, example_count))], axis=0)
        share = gram.shape[0] // devices
        summed = jnp.sum(swap(gram, EVERY).reshape(devices, share, example_count), axis=0)
        pieces = swap(jnp.broadcast_to(summed[None], (devices, share, example_count)), EVERY)
        pieces = pieces.reshape(1, devices * share, example_count)
    scores, domain_scores = solve(pieces, target_ids, slot, ex_rows, example_count)
    return (scores.T, domain_scores.T)


def solution(mesh):
    in_specs = (
        P("ex", None, "param"),
        P(None, "ex", None, "param"),
        P(None, None, "param"),
        P(None, "param", None),
        P(("param", "ex"), None),
        P("ex"),
        P("param"),
    )
    out_specs = (P("param", "ex"), P("param", None))
    return jax.shard_map(local, mesh=mesh, in_specs=in_specs, out_specs=out_specs, check_vma=False)
```
